256 devices in a mesh: gx: 8 (over y, core), gy: 32 (over z, x).
Axes of the slice: x: 4, y: 4, z: 8, core: 2. Of those that a mesh axis runs over, the one named last changes fastest.
Arguments:
- state_mean: float32 [2, 512, 1024], P(None, 'gy', 'gx'), may hold values from -6 to 6
- state_spread: bfloat16 [2, 512, 1024, 128], P(None, 'gy', 'gx'), may hold values from -6 to 6
- obs_value: float32 [2, 8, 32, 4], replicated, may hold values from -8 to 8
- obs_var: float32 [2, 8, 32, 4], replicated, may hold values from 0.25 to 4
- obs_col: int32 [2, 8, 32, 4], replicated, may hold values from 0 to 127
- obs_row: int32 [2, 8, 32, 4], replicated, may hold values from 0 to 15
- obs_level: int32 [2, 8, 32, 4], replicated, may hold values from 0 to 1
Outputs:
- analysis_mean: float32 [2, 512, 1024], P(None, 'gy', 'gx')
- analysis_spread: bfloat16 [2, 512, 1024, 128], P(None, 'gy', 'gx')
The draws below stay inside these ranges and needn't reach their ends.
All inputs are finite; a program needn't handle non-finite values.
Results may differ from the reference program's by a relative error of at most 0.011.
Values may be sent and summed in bfloat16 or wider, within the bound.
A program may use at most 64 MiB of HBM per device.

```python
import math
import jax
import jax.numpy as jnp
from jax import lax

CX = 128
CY = 16
LEV = 2
M = 128
OBS_DEV = 4
NB = 2
NX = 1024
NY = 512
LOC = 512
N_GX = 8
N_GY = 32


def place_ends(values, stream_key, least, largest):
    dims = values.shape
    place = [jax.random.randint(jax.random.fold_in(stream_key, axis), (), 0, dims[axis]) for axis in range(len(dims))]
    values = values.at[tuple(place)].set(least)
    longest = dims.index(max(dims))
    place[longest] = (place[longest] + 1) % dims[longest]
    return values.at[tuple(place)].set(largest)


def shard_levels(key, dims, cuts, smallest, top_value):
    factor_of, own = 1.0, jax.random.fold_in(key, 6)
    for dim, blocks in cuts:
        steps = jnp.exp(jax.random.uniform(jax.random.fold_in(own, dim), (blocks,), jnp.float32, smallest / len(cuts), top_value / len(cuts)))
        factor_of = factor_of * jnp.repeat(steps, dims[dim] // blocks).reshape([-1 if axis == dim else 1 for axis in range(len(dims))])
    return factor_of


def scatter_about(own_key, shape, scale, most, pieces=(), held_as=jnp.bfloat16):
    array = scale * jax.random.normal(own_key, shape, jnp.float32)
    if pieces:
        array = array * shard_levels(own_key, shape, pieces, -0.22, 0.18)
    return jnp.clip(array, -most, most).astype(held_as)


def setup_inputs(seed: int = 0) -> dict:
    keys = jax.random.split(jax.random.key(seed), 8)
    state_mean = scatter_about(keys[0], (LEV, NY, NX), 1.0, 6.0, ((1, 32), (2, 8)), jnp.float32)
    state_spread = scatter_about(keys[1], (LEV, NY, NX, M), 1.0, 6.0, ((1, 32), (2, 8)))
    obs_value = scatter_about(keys[2], (NB, N_GX, N_GY, OBS_DEV), 1.5, 8.0, (), jnp.float32)
    obs_var = jnp.clip(jnp.exp(jax.random.uniform(keys[3], (NB, N_GX, N_GY, OBS_DEV), jnp.float32, math.log(0.25), math.log(4.0))), 0.25, 4.0)
    obs_col = place_ends(jax.random.randint(keys[4], (NB, N_GX, N_GY, OBS_DEV), 0, CX), jax.random.fold_in(keys[4], 1), 0, CX - 1).astype(jnp.int32)
    obs_row = place_ends(jax.random.randint(keys[5], (NB, N_GX, N_GY, OBS_DEV), 0, CY), jax.random.fold_in(keys[5], 1), 0, CY - 1).astype(jnp.int32)
    obs_level = place_ends(jax.random.randint(keys[6], (NB, N_GX, N_GY, OBS_DEV), 0, LEV), jax.random.fold_in(keys[6], 1), 0, LEV - 1).astype(jnp.int32)
    return {"state_mean": state_mean, "state_spread": state_spread, "obs_value": obs_value, "obs_var": obs_var, "obs_col": obs_col, "obs_row": obs_row, "obs_level": obs_level}


PRECISE = lax.Precision.HIGHEST

def taper(dist_sq, radius):
    ratio = jnp.sqrt(dist_sq) / radius
    ratio_safe = jnp.maximum(ratio, 1.0)
    inner_part = (((-0.25 * ratio + 0.5) * ratio + 0.625) * ratio - 5.0 / 3.0) * ratio * ratio + 1.0
    outer_part = ((((ratio / 12.0 - 0.5) * ratio + 0.625) * ratio + 5.0 / 3.0) * ratio - 5.0) * ratio + 4.0 - 2.0 / (3.0 * ratio_safe)
    return jnp.where(ratio <= 1.0, inner_part, jnp.where(ratio < 2.0, outer_part, 0.0))

def reference(state_mean, state_spread, obs_value, obs_var, obs_col, obs_row, obs_level):
    root_dof = jnp.sqrt(jnp.float32(M - 1))
    mean_now = state_mean
    spread = state_spread
    item_count = LEV * NY // 8
    for block_idx in range(NB):
        obs_x = (jnp.arange(N_GX, dtype=jnp.int32)[:, None, None] * CX + obs_col[block_idx]).reshape(-1)
        obs_y = (jnp.arange(N_GY, dtype=jnp.int32)[None, :, None] * CY + obs_row[block_idx]).reshape(-1)
        obs_lev = obs_level[block_idx].reshape(-1)
        prior_obs = mean_now[obs_lev, obs_y, obs_x]
        panel_z = spread[obs_lev, obs_y, obs_x, :].astype(jnp.float32)
        obs_sd = jnp.sqrt(obs_var[block_idx].reshape(-1))
        weighted = panel_z / (obs_sd[:, None] * root_dof)
        innov_norm = (obs_value[block_idx].reshape(-1) - prior_obs) / obs_sd
        gram = jnp.eye(M, dtype=jnp.float32) + jnp.dot(weighted.T, weighted, precision=PRECISE)
        proj = jnp.dot(weighted.T, innov_norm, precision=PRECISE)
        factor = jnp.linalg.cholesky(gram)
        ens_weights = jax.scipy.linalg.cho_solve((factor, True), proj)
        panel_e = (innov_norm - jnp.dot(weighted, ens_weights, precision=PRECISE)) / obs_sd
        solved = jax.scipy.linalg.cho_solve((factor, True), weighted.T)
        panel_q = (root_dof / obs_sd)[:, None] * solved.T
        panel_zb = panel_z.astype(jnp.bfloat16)
        panel_qb = panel_q.astype(jnp.bfloat16)
        panel_eb = panel_e.astype(jnp.bfloat16)
        spread_items = spread.reshape(item_count, 8 * NX, M)
        mean_items = mean_now.reshape(item_count, 8 * NX)

        def update(operands):
            item_idx, spread_blk, mean_blk = operands
            local_ids = jnp.arange(8 * NX, dtype=jnp.int32)
            row_ids = item_idx % (NY // 8) * 8 + local_ids // NX
            col_ids = local_ids % NX
            delta_x = (col_ids[:, None] - obs_x[None, :]).astype(jnp.float32)
            delta_y = (row_ids[:, None] - obs_y[None, :]).astype(jnp.float32)
            taper_vals = taper(delta_x * delta_x + delta_y * delta_y, LOC)
            covariance = jnp.dot(spread_blk.astype(jnp.float32), panel_zb.T.astype(jnp.float32), preferred_element_type=jnp.float32) / (M - 1.0)
            gain_bf = (taper_vals * covariance).astype(jnp.bfloat16)
            new_mean = mean_blk + jnp.dot(gain_bf.astype(jnp.float32), panel_eb.astype(jnp.float32), preferred_element_type=jnp.float32)
            new_spread = (spread_blk.astype(jnp.float32) - 0.5 * jnp.dot(gain_bf.astype(jnp.float32), panel_qb.astype(jnp.float32), preferred_element_type=jnp.float32)).astype(jnp.bfloat16)
            return (new_mean, new_spread)
        new_means, new_spreads = lax.map(update, (jnp.arange(item_count, dtype=jnp.int32), spread_items, mean_items))
        mean_now = new_means.reshape(LEV, NY, NX)
        spread = new_spreads.reshape(LEV, NY, NX, M)
    return (mean_now, spread)
```

```python
import functools
import jax
import jax.numpy as jnp
from jax import lax
from jax.experimental import pallas as pl
from jax.experimental.pallas import tpu as pltpu
from jax.sharding import PartitionSpec as P

MESH = pl.DeviceIdType.MESH


def gather_kernel(nx, ny, cells_x, spread_hbm, mean_ref, idx_ref, z_ref, p_ref,
                  cells, send, rows, near, pnear, allz, allp,
                  load_sem, self_sem, send_sem, recv_sem, zsend, zrecv, psend, precv):
    ax = lax.axis_index("gx")
    ay = lax.axis_index("gy")
    load = pltpu.make_async_copy(spread_hbm, cells, load_sem)
    load.start()
    other = ax + 1 - 2 * lax.rem(ax, 2)
    barrier = pltpu.get_barrier_semaphore()

    def greet(o, carry):
        pl.semaphore_signal(barrier, inc=1, device_id=(ax, lax.rem(ay + o, ny)), device_id_type=MESH)
        return carry

    lax.fori_loop(1, ny, greet, 0)

    def greet_y(o, carry):
        pl.semaphore_signal(barrier, inc=1, device_id=(lax.rem(ax + o, nx), ay), device_id_type=MESH)
        return carry

    lax.fori_loop(1, nx, greet_y, 0)

    members = cells.shape[2]
    sub = lax.broadcasted_iota(jnp.int32, (16, members), 0)
    lane = lax.broadcasted_iota(jnp.int32, (1, members), 1)
    place = (lax.broadcasted_iota(jnp.int32, mean_ref.shape, 0) * cells_x
             + lax.broadcasted_iota(jnp.int32, mean_ref.shape, 1))
    load.wait()
    prior = []
    for b in range(2):
        prow = jnp.zeros((1, members), jnp.float32)
        for s in range(4):
            f = idx_ref[((b * nx + ax) * ny + ay) * 4 + s]
            tile = cells[f >> 4].astype(jnp.float32)
            row = jnp.sum(jnp.where(sub == (f & 15), tile, 0.0), axis=0, keepdims=True)
            rows[b * 4 + s:b * 4 + s + 1, :] = row
            val = jnp.where(place == f, mean_ref[...], 0.0)
            val = jnp.sum(jnp.sum(val, axis=0, keepdims=True), axis=1, keepdims=True)
            prow = prow + jnp.where(lane == 4 * ay + s, jnp.broadcast_to(val, (1, members)), 0.0)
        prior.append(prow)
    send[0] = rows[0:4, :].astype(jnp.bfloat16)
    send[1] = rows[4:8, :].astype(jnp.bfloat16)
    for b in range(2):
        hi = prior[b].astype(jnp.bfloat16).astype(jnp.float32)
        rows[2 * b:2 * b + 1, :] = hi
        rows[2 * b + 1:2 * b + 2, :] = prior[b] - hi
    send[2] = rows[0:4, :].astype(jnp.bfloat16)
    pl.semaphore_wait(barrier, ny - 1 + nx - 1)

    own = pltpu.make_async_copy(send, near.at[:, ay], self_sem.at[0])
    own.start()

    def spread_out(o, carry):
        to = lax.rem(ay + o, ny)
        pltpu.make_async_remote_copy(
            send, near.at[:, ay], send_sem.at[to], recv_sem.at[ay],
            device_id=(ax, to), device_id_type=MESH).start()
        return carry

    lax.fori_loop(1, ny, spread_out, 0)
    own.wait()

    def arrive(o, carry):
        frm = lax.rem(ay + o, ny)
        pltpu.make_async_remote_copy(
            send, near.at[:, frm], send_sem.at[frm], recv_sem.at[frm],
            device_id=(ax, frm), device_id_type=MESH).wait()
        return carry

    lax.fori_loop(1, ny, arrive, 0)

    keep = pltpu.make_async_copy(near.at[0:2], allz.at[ax], self_sem.at[1])
    keep.start()

    def zcopy(src, slot, to):
        return pltpu.make_async_remote_copy(src, allz.at[slot], zsend.at[slot], zrecv.at[slot],
                                            device_id=(to, ay), device_id_type=MESH)

    def zout(o, carry):
        to = lax.rem(ax + 2 * o, nx)
        pltpu.make_async_remote_copy(near.at[0:2], allz.at[ax], zsend.at[to], zrecv.at[ax],
                                     device_id=(to, ay), device_id_type=MESH).start()
        return carry

    lax.fori_loop(1, nx // 2, zout, 0)
    pltpu.make_async_remote_copy(near.at[0:2], allz.at[ax], zsend.at[other], zrecv.at[ax],
                                 device_id=(other, ay), device_id_type=MESH).start()
    ptile = near[2].astype(jnp.float32)
    psum = jnp.sum(ptile, axis=0)
    pnear[0:1, :] = psum[0:1, :] + psum[1:2, :]
    pnear[1:2, :] = psum[2:3, :] + psum[3:4, :]
    allp[ax] = pnear[...]

    def pout(o, carry):
        to = lax.rem(ax + o, nx)
        pltpu.make_async_remote_copy(pnear, allp.at[ax], psend.at[to], precv.at[ax],
                                     device_id=(to, ay), device_id_type=MESH).start()
        return carry

    lax.fori_loop(1, nx, pout, 0)

    def relay(o, carry):
        g = lax.rem(ax + 2 * o, nx)
        pltpu.make_async_remote_copy(near.at[0:2], allz.at[g], zsend.at[g], zrecv.at[g],
                                     device_id=(g, ay), device_id_type=MESH).wait()
        pltpu.make_async_remote_copy(allz.at[g], allz.at[g], zsend.at[lax.rem(g + 1 - 2 * lax.rem(g, 2) + nx, nx)],
                                     zrecv.at[g], device_id=(other, ay), device_id_type=MESH).start()
        return carry

    lax.fori_loop(1, nx // 2, relay, 0)

    def settle(o, carry):
        g = lax.rem(ax + 2 * o, nx)
        h = g + 1 - 2 * lax.rem(g, 2)
        pltpu.make_async_remote_copy(allz.at[h], allz.at[h], zsend.at[h], zrecv.at[h],
                                     device_id=(other, ay), device_id_type=MESH).wait()
        return carry

    lax.fori_loop(0, nx // 2, settle, 0)

    def settle_p(o, carry):
        g = lax.rem(ax + o, nx)
        pltpu.make_async_remote_copy(pnear, allp.at[g], psend.at[g], precv.at[g],
                                     device_id=(g, ay), device_id_type=MESH).wait()
        return carry

    lax.fori_loop(1, nx, settle_p, 0)
    keep.wait()
    p_ref[...] = allp[...]
    outs = [pltpu.make_async_copy(allz.at[:, b], z_ref.at[b], self_sem.at[b]) for b in range(2)]
    for c in outs:
        c.start()
    for c in outs:
        c.wait()


def gather(nx, ny, spread, mean, idx):
    members = spread.shape[2]
    cells_x = mean.shape[1]
    bf, f32 = jnp.bfloat16, jnp.float32
    vm = pl.BlockSpec(memory_space=pltpu.VMEM)
    dma = pltpu.SemaphoreType.DMA
    return pl.pallas_call(
        functools.partial(gather_kernel, nx, ny, cells_x),
        out_shape=(jax.ShapeDtypeStruct((2, nx, ny, 4, members), bf), jax.ShapeDtypeStruct((nx, 8, members), f32)),
        in_specs=[pl.BlockSpec(memory_space=pl.ANY), vm, pl.BlockSpec(memory_space=pltpu.SMEM)],
        out_specs=(pl.BlockSpec(memory_space=pl.ANY), vm),
        scratch_shapes=[
            pltpu.VMEM(spread.shape, bf),
            pltpu.VMEM((3, 4, members), bf),
            pltpu.VMEM((8, members), f32),
            pltpu.VMEM((3, ny, 4, members), bf),
            pltpu.VMEM((8, members), f32),
            pltpu.VMEM((nx, 2, ny, 4, members), bf),
            pltpu.VMEM((nx, 8, members), f32),
            dma, dma((2,)), dma((ny,)), dma((ny,)), dma((nx,)), dma((nx,)), dma((nx,)), dma((nx,)),
        ],
        compiler_params=pltpu.CompilerParams(collective_id=0, has_side_effects=True, vmem_limit_bytes=60 << 20),
    )(spread, mean, idx)


HI = lax.Precision.HIGHEST
BF = jnp.bfloat16
F32 = jnp.float32


def mm(a, b):
    return jnp.dot(a, b, preferred_element_type=F32)


def split3(x):
    a = x.astype(BF)
    r = x - a.astype(F32)
    b = r.astype(BF)
    return a, b, (r - b.astype(F32)).astype(BF)


def taper_scaled(t, scale):
    rs = lax.rsqrt(t)
    r = t * rs
    c = scale
    inner = (((-0.25 * c * r + 0.5 * c) * r + 0.625 * c) * r - 5.0 / 3.0 * c) * t + c
    m = jnp.maximum(2.0 - r, 0.0)
    m = m * m
    m = m * m
    outer = m * ((r * (c / 12.0) + c / 6.0) - rs * (c / 24.0))
    return jnp.where(t <= 1.0, inner, outer)


def columns(row, out):
    for i in range(row.shape[1] // 128):
        tile = jnp.broadcast_to(row[:, i * 128:(i + 1) * 128], (128, 128))
        out[i * 128:(i + 1) * 128, :] = tile.T


def chain(zx, zt, qx, dcol, ivcol, z_f32, ivar_row):
    count, members = z_f32.shape
    dof = members - 1.0
    lane = lax.broadcasted_iota(jnp.int32, (count, members), 1)
    d1, d2, d3 = split3(dcol[...])
    zero = jnp.zeros((), BF)
    zx[:, :members] = z_f32.astype(BF)
    zx[:, members:] = jnp.where(lane == 0, d1.astype(F32), jnp.where(
        lane == 1, d2.astype(F32), jnp.where(lane == 2, d3.astype(F32), 0.0))).astype(BF)
    z_t = z_f32.T
    zt[...] = z_t.astype(BF)
    h1, h2, h3 = split3(z_t * (ivar_row * (1.0 / dof)))
    rhs = zx[...]
    full = mm(h1, rhs) + mm(h2, rhs) + mm(h3, rhs)
    row_i = lax.broadcasted_iota(jnp.int32, (members, members), 0)
    col_i = lax.broadcasted_iota(jnp.int32, (members, members), 1)
    eye = jnp.where(row_i == col_i, 1.0, 0.0).astype(F32)
    gram = full[:, :members] + eye
    vec = jnp.broadcast_to(jnp.sum(full[:, members:], axis=1, keepdims=True), (members, members))
    top = jnp.max(jnp.sum(jnp.abs(gram), axis=1, keepdims=True))
    scale = 2.0 / (1.0 + top)
    first = scale * (2.0 * eye - scale * gram)

    def more(state):
        step, miss, _ = state
        return jnp.logical_and(step < 60, miss > 1e-3)

    def newton(state):
        step, _, x = state
        resid = eye - jnp.dot(gram, x, precision=HI, preferred_element_type=F32)
        x = x + jnp.dot(x, resid, precision=HI, preferred_element_type=F32)
        return step + 1, jnp.max(jnp.abs(resid)), x

    _, _, inv = lax.while_loop(more, newton, (jnp.int32(0), jnp.float32(1.0), first))
    w = jnp.dot(inv, vec, precision=HI, preferred_element_type=F32)
    r1, r2, r3 = split3(jnp.concatenate([inv, -w], axis=1))
    row_e = lax.broadcasted_iota(jnp.int32, (members, 2 * members), 0)
    col_e = lax.broadcasted_iota(jnp.int32, (members, 2 * members), 1)
    ones = jnp.where(jnp.logical_and(row_e < 3, col_e >= members), 1.0, 0.0).astype(BF)
    z_b = rhs[:, :members]
    acc = mm(rhs, jnp.concatenate([r1, ones], axis=0)) + mm(z_b, r2) + mm(z_b, r3)
    iv = ivcol[...]
    qx[...] = (acc * jnp.concatenate([iv, iv], axis=1)).astype(BF)


def update_kernel(nx, ny, radius, spread_ref, mean_ref, z_ref, p_ref, meta_ref, mean_out, spread_out,
                  zx, zt, qx, z1, dcol, ivcol, xcol, ycol, dx2, macc):
    ax = lax.axis_index("gx")
    ay = lax.axis_index("gy")
    levels, rows_y, cols_x, members = spread_ref.shape
    count = z1.shape[0]
    inv_sq = 1.0 / (radius * radius)
    unit = 1.0 / (members - 1.0)
    prior = [jnp.concatenate([p_ref[i, b:b + 1, :] for i in range(nx)], axis=1) for b in range(2)]
    meta = [[meta_ref[4 * b + c:4 * b + c + 1, :] for c in range(4)] for b in range(2)]
    columns(meta[0][3] - prior[0], dcol)
    columns(1.0 / meta[0][2], ivcol)
    chain(zx, zt.at[0], qx.at[0], dcol, ivcol, z_ref[0].astype(F32).reshape(count, members), 1.0 / meta[0][2])
    columns(meta[1][3] - prior[1], dcol)
    columns(1.0 / meta[1][2], ivcol)
    columns(meta[1][0], xcol)
    columns(meta[1][1], ycol)
    z1[...] = z_ref[1].astype(F32).reshape(count, members).astype(BF)

    def cross(c, carry):
        rows = pl.ds(pl.multiple_of(c * 128, 128), 128)
        x_c, y_c = xcol[rows, :], ycol[rows, :]
        parts = []
        z_c = z1[rows, :]
        for i in range(count // 128):
            cut = slice(i * 128, (i + 1) * 128)
            ddx = x_c - meta[0][0][:, cut]
            ddy = y_c - meta[0][1][:, cut]
            t = (ddx * ddx + ddy * ddy) * inv_sq + 1e-30
            cov = mm(z_c, zt[0, :, cut])
            parts.append((taper_scaled(t, unit) * cov).astype(BF))
        inc = mm(jnp.concatenate(parts, axis=1), qx[0])
        z1[rows, :] = (z_c.astype(F32) - 0.5 * inc[:, :members]).astype(BF)
        dcol[rows, :] = dcol[rows, :] - inc[:, members:]
        return carry

    lax.fori_loop(0, count // 128, cross, 0)
    chain(zx, zt.at[1], qx.at[1], dcol, ivcol, z1[...].astype(F32), 1.0 / meta[1][2])

    col_x = (ax * cols_x + lax.broadcasted_iota(jnp.int32, (cols_x, 1), 0)).astype(F32)
    for b in range(2):
        ddx = col_x - meta[b][0]
        dx2[b] = ddx * ddx * inv_sq + 1e-30
    macc[...] = jnp.zeros_like(macc)
    lane = lax.broadcasted_iota(jnp.int32, (cols_x, members), 1)

    def sweep(y, carry):
        here = (ay * rows_y + y).astype(F32)
        s = [spread_ref[lev, y] for lev in range(levels)]
        for b in range(2):
            ddy = here - meta[b][1]
            dy2 = ddy * ddy * inv_sq
            parts = [[] for _ in range(levels)]
            for i in range(count // 128):
                cut = slice(i * 128, (i + 1) * 128)
                tap = taper_scaled(dx2[b, :, cut] + dy2[:, cut], unit)
                for lev in range(levels):
                    cov = mm(s[lev], zt[b, :, cut])
                    parts[lev].append((tap * cov).astype(BF))
            for lev in range(levels):
                inc = mm(jnp.concatenate(parts[lev], axis=1), qx[b])
                s[lev] = (s[lev].astype(F32) - 0.5 * inc[:, :members]).astype(BF)
                macc[...] += jnp.where(lane == lev * rows_y + y, inc[:, members:], 0.0)
        for lev in range(levels):
            spread_out[lev, y] = s[lev]
        return carry

    lax.fori_loop(0, rows_y, sweep, 0)
    mean_out[...] = mean_ref[...] + macc[...].T[:levels * rows_y, :]


def update(nx, ny, radius, spread, mean, z, p, meta):
    levels, rows_y, cols_x, members = spread.shape
    count = meta.shape[1]
    vm = pl.BlockSpec(memory_space=pltpu.VMEM)
    return pl.pallas_call(
        functools.partial(update_kernel, nx, ny, radius),
        out_shape=(jax.ShapeDtypeStruct(mean.shape, F32), jax.ShapeDtypeStruct(spread.shape, BF)),
        in_specs=[vm] * 5,
        out_specs=(vm, vm),
        scratch_shapes=[
            pltpu.VMEM((count, 2 * members), BF),
            pltpu.VMEM((2, members, count), BF),
            pltpu.VMEM((2, count, 2 * members), BF),
            pltpu.VMEM((count, members), BF),
            pltpu.VMEM((count, members), F32),
            pltpu.VMEM((count, members), F32),
            pltpu.VMEM((count, members), F32),
            pltpu.VMEM((count, members), F32),
            pltpu.VMEM((2, cols_x, count), F32),
            pltpu.VMEM((cols_x, members), F32),
        ],
        compiler_params=pltpu.CompilerParams(vmem_limit_bytes=60 << 20),
    )(spread, mean, z, p, meta)


def body(state_mean, state_spread, obs_value, obs_var, obs_col, obs_row, obs_level):
    levels, rows_y, cols_x, members = state_spread.shape
    nx, ny = lax.axis_size("gx"), lax.axis_size("gy")
    radius = nx * cols_x // 2
    spread = state_spread.reshape(levels * rows_y * cols_x // 16, 16, members)
    mean = state_mean.reshape(levels * rows_y, cols_x)
    idx = ((obs_level * rows_y + obs_row) * cols_x + obs_col).reshape(-1)
    z, p = gather(nx, ny, spread, mean, idx)
    obs_x = (jnp.arange(nx, dtype=jnp.int32)[None, :, None, None] * cols_x + obs_col).astype(F32)
    obs_y = (jnp.arange(ny, dtype=jnp.int32)[None, None, :, None] * rows_y + obs_row).astype(F32)
    meta = jnp.stack([obs_x, obs_y, obs_var, obs_value], axis=1).reshape(8, -1)
    new_mean, new_spread = update(nx, ny, radius, state_spread, mean, z, p, meta)
    return new_mean.reshape(state_mean.shape), new_spread


def solution(mesh):
    return jax.shard_map(
        body,
        mesh=mesh,
        in_specs=(P(None, "gy", "gx"), P(None, "gy", "gx", None), P(), P(), P(), P(), P()),
        out_specs=(P(None, "gy", "gx"), P(None, "gy", "gx", None)),
        check_vma=False,
    )
```

```python
import functools
import jax
import jax.numpy as jnp
from jax import lax
from jax.experimental import pallas as pl
from jax.experimental.pallas import tpu as pltpu
from jax.sharding import PartitionSpec as P

MESH = pl.DeviceIdType.MESH
HI = lax.Precision.HIGHEST
BF = jnp.bfloat16
F32 = jnp.float32
PER = 4
SPLIT = (4, 20, 12)


def mm(a, b):
    return jnp.dot(a, b, preferred_element_type=F32)


def exact(a, b):
    return jnp.dot(a, b, precision=HI, preferred_element_type=F32)


def split3(x):
    a = x.astype(BF)
    r = x - a.astype(F32)
    b = r.astype(BF)
    return a, b, (r - b.astype(F32)).astype(BF)


def taper_scaled(t, c):
    rs = lax.rsqrt(t)
    r = t * rs
    inner = (((-0.25 * c * r + 0.5 * c) * r + 0.625 * c) * r - 5.0 / 3.0 * c) * t + c
    m = jnp.maximum(2.0 - r, 0.0)
    m = m * m
    m = m * m
    outer = m * ((r * (c / 12.0) + c / 6.0) - rs * (c / 24.0))
    return jnp.where(t <= 1.0, inner, outer)


def columns(rows8, out):
    turned = jnp.broadcast_to(rows8[:, None, :], (8, 16, 128)).reshape(128, 128).T
    for i in range(8):
        out[i * 128:(i + 1) * 128, :] = jnp.broadcast_to(turned[:, 16 * i:16 * i + 1], (128, 128))


def wide(rows8):
    return jnp.concatenate([rows8[i:i + 1, :] for i in range(8)], axis=1)


def gather_kernel(nx, ny, radius, cols_x, rows_y, spread_hbm, mean_ref, col_ref, row_ref, lev_ref, var_ref, val_ref,
                  z_ref, p_ref, meta_ref, tap_ref,
                  cells, send, rows, near, pnear, allz, allp, dx2, xcol, ycol, tap,
                  load_sem, self_sem, tap_sem, send_sem, recv_sem, zsend, zrecv, psend, precv):
    ax = lax.axis_index("gx")
    ay = lax.axis_index("gy")
    load = pltpu.make_async_copy(spread_hbm, cells, load_sem)
    load.start()
    other = ax + 1 - 2 * lax.rem(ax, 2)
    barrier = pltpu.get_barrier_semaphore()

    def greet(o, carry):
        pl.semaphore_signal(barrier, inc=1, device_id=(ax, lax.rem(ay + o, ny)), device_id_type=MESH)
        return carry

    lax.fori_loop(1, ny, greet, 0)

    def greet_x(o, carry):
        pl.semaphore_signal(barrier, inc=1, device_id=(lax.rem(ax + o, nx), ay), device_id_type=MESH)
        return carry

    lax.fori_loop(1, nx, greet_x, 0)

    members = cells.shape[1]
    total = cells.shape[0]
    lane = lax.broadcasted_iota(jnp.int32, (1, members), 1)
    place = (lax.broadcasted_iota(jnp.int32, mean_ref.shape, 0) * cols_x
             + lax.broadcasted_iota(jnp.int32, mean_ref.shape, 1)).astype(F32)

    mine = []
    for b in range(2):
        at = b * nx + ax
        flat = (lev_ref[at] * rows_y + row_ref[at]) * cols_x + col_ref[at]
        pick = lax.broadcasted_iota(jnp.int32, flat.shape, 1) == ay
        mine.append(jnp.sum(jnp.where(pick, flat.astype(F32), 0.0), axis=1, keepdims=True))
    mine = jnp.concatenate(mine, axis=0)
    ids = lax.broadcasted_iota(jnp.int32, (2 * PER, total), 1).astype(F32)
    hot = jnp.where(ids == mine, 1.0, 0.0).astype(BF)
    prior = []
    for b in range(2):
        prow = jnp.zeros((1, members), F32)
        for s in range(PER):
            f = mine[b * PER + s:b * PER + s + 1, :]
            v = jnp.where(place == f, mean_ref[...], 0.0)
            v = jnp.sum(jnp.sum(v, axis=0, keepdims=True), axis=1, keepdims=True)
            prow = prow + jnp.where(lane == ny * s + ay, jnp.broadcast_to(v, (1, members)), 0.0)
        prior.append(prow)
    for b in range(2):
        hi = prior[b].astype(BF).astype(F32)
        rows[2 * b:2 * b + 1, :] = hi
        rows[2 * b + 1:2 * b + 2, :] = prior[b] - hi
    send[2] = rows[0:4, :].astype(BF)
    load.wait()
    rows[...] = mm(hot, cells[...])
    send[0] = rows[0:4, :].astype(BF)
    send[1] = rows[4:8, :].astype(BF)

    def flatten(ref, bias):
        acc = jnp.zeros((2 * nx, members), F32)
        for s in range(PER):
            spot = jnp.where(lax.broadcasted_iota(jnp.int32, (ny, members), 1)
                             == lax.broadcasted_iota(jnp.int32, (ny, members), 0) + ny * s, 1.0, 0.0)
            acc = acc + exact(ref[:, s, :].astype(F32), spot.astype(F32))
        return acc + bias

    group = lax.rem(lax.broadcasted_iota(jnp.int32, (2 * nx, members), 0), nx)
    strip = lax.rem(lax.broadcasted_iota(jnp.int32, (2 * nx, members), 1), ny)
    meta_ref[0] = flatten(col_ref, (group * cols_x).astype(F32))
    meta_ref[1] = flatten(row_ref, (strip * rows_y).astype(F32))
    meta_ref[2] = flatten(var_ref, 0.0)
    meta_ref[3] = flatten(val_ref, 0.0)

    inv_sq = 1.0 / (radius * radius)
    unit = 1.0 / (members - 1.0)
    col_x = (ax * cols_x + lax.broadcasted_iota(jnp.int32, (cols_x, 1), 0)).astype(F32)
    for b in range(2):
        ddx = col_x - wide(meta_ref[0, b * nx:(b + 1) * nx, :])
        dx2[b] = ddx * ddx * inv_sq + 1e-30
    columns(meta_ref[0, nx:2 * nx, :], xcol)
    columns(meta_ref[1, nx:2 * nx, :], ycol)

    def ship(n):
        pltpu.make_async_copy(tap.at[n], tap_ref.at[n], tap_sem).start()

    def cross_tile(i, carry):
        r = pl.ds(pl.multiple_of(i * 128, 128), 128)
        x_c, y_c = xcol[r, :], ycol[r, :]
        for c in range(nx):
            ddx = x_c - meta_ref[0, c:c + 1, :]
            ddy = y_c - meta_ref[1, c:c + 1, :]
            t = (ddx * ddx + ddy * ddy) * inv_sq + 1e-30
            tap[i, :, c * 128:(c + 1) * 128] = taper_scaled(t, unit)
        ship(i)
        return carry

    def own_tile(n, carry):
        b = n // rows_y
        here = (ay * rows_y + lax.rem(n, rows_y)).astype(F32)
        for c in range(nx):
            ddy = here - meta_ref[1, pl.ds(b * nx + c, 1), :]
            t = dx2[b, :, c * 128:(c + 1) * 128] + ddy * ddy * inv_sq
            tap[nx + n, :, c * 128:(c + 1) * 128] = taper_scaled(t, unit)
        ship(nx + n)
        return carry

    first, second, third = SPLIT
    lax.fori_loop(0, first, cross_tile, 0)
    pl.semaphore_wait(barrier, ny - 1 + nx - 1)

    own = pltpu.make_async_copy(send, near.at[:, ay], self_sem.at[0])
    own.start()

    def spread_out(o, carry):
        to = lax.rem(ay + o, ny)
        pltpu.make_async_remote_copy(
            send, near.at[:, ay], send_sem.at[to], recv_sem.at[ay],
            device_id=(ax, to), device_id_type=MESH).start()
        return carry

    lax.fori_loop(1, ny, spread_out, 0)
    lax.fori_loop(first, nx, cross_tile, 0)
    lax.fori_loop(0, second - (nx - first), own_tile, 0)
    own.wait()

    def arrive(o, carry):
        frm = lax.rem(ay + o, ny)
        pltpu.make_async_remote_copy(
            send, near.at[:, frm], send_sem.at[frm], recv_sem.at[frm],
            device_id=(ax, frm), device_id_type=MESH).wait()
        return carry

    lax.fori_loop(1, ny, arrive, 0)

    keep = pltpu.make_async_copy(near.at[0:2], allz.at[ax], self_sem.at[1])
    keep.start()

    def zout(o, carry):
        to = lax.rem(ax + 2 * o, nx)
        pltpu.make_async_remote_copy(near.at[0:2], allz.at[ax], zsend.at[to], zrecv.at[ax],
                                     device_id=(to, ay), device_id_type=MESH).start()
        return carry

    lax.fori_loop(1, nx // 2, zout, 0)
    pltpu.make_async_remote_copy(near.at[0:2], allz.at[ax], zsend.at[other], zrecv.at[ax],
                                 device_id=(other, ay), device_id_type=MESH).start()
    psum = jnp.sum(near[2].astype(F32), axis=0)
    pnear[0:1, :] = psum[0:1, :] + psum[1:2, :]
    pnear[1:2, :] = psum[2:3, :] + psum[3:4, :]
    allp[ax] = pnear[...]

    def pout(o, carry):
        to = lax.rem(ax + o, nx)
        pltpu.make_async_remote_copy(pnear, allp.at[ax], psend.at[to], precv.at[ax],
                                     device_id=(to, ay), device_id_type=MESH).start()
        return carry

    lax.fori_loop(1, nx, pout, 0)
    lax.fori_loop(second - (nx - first), second - (nx - first) + third, own_tile, 0)

    def relay(o, carry):
        g = lax.rem(ax + 2 * o, nx)
        h = g + 1 - 2 * lax.rem(g, 2)
        pltpu.make_async_remote_copy(near.at[0:2], allz.at[g], zsend.at[g], zrecv.at[g],
                                     device_id=(g, ay), device_id_type=MESH).wait()
        pltpu.make_async_remote_copy(allz.at[g], allz.at[g], zsend.at[h], zrecv.at[g],
                                     device_id=(other, ay), device_id_type=MESH).start()
        return carry

    lax.fori_loop(1, nx // 2, relay, 0)
    lax.fori_loop(second - (nx - first) + third, 2 * rows_y, own_tile, 0)

    def settle(o, carry):
        g = lax.rem(ax + 2 * o, nx)
        h = g + 1 - 2 * lax.rem(g, 2)
        pltpu.make_async_remote_copy(allz.at[h], allz.at[h], zsend.at[h], zrecv.at[h],
                                     device_id=(other, ay), device_id_type=MESH).wait()
        return carry

    lax.fori_loop(0, nx // 2, settle, 0)

    def settle_p(o, carry):
        g = lax.rem(ax + o, nx)
        pltpu.make_async_remote_copy(pnear, allp.at[g], psend.at[g], precv.at[g],
                                     device_id=(g, ay), device_id_type=MESH).wait()
        return carry

    lax.fori_loop(1, nx, settle_p, 0)
    keep.wait()
    p_ref[...] = allp[...]
    outs = [pltpu.make_async_copy(allz.at[:, b], z_ref.at[b], self_sem.at[b]) for b in range(2)]
    for c in outs:
        c.start()
    for c in outs:
        c.wait()
    pltpu.make_async_copy(tap, tap_ref, tap_sem).wait()


def gather(nx, ny, radius, cols_x, rows_y, spread, mean, col, row, lev, var, val):
    members = spread.shape[1]
    count = nx * ny * PER
    tiles = nx + 2 * rows_y
    vm = pl.BlockSpec(memory_space=pltpu.VMEM)
    hbm = pl.BlockSpec(memory_space=pl.ANY)
    dma = pltpu.SemaphoreType.DMA
    return pl.pallas_call(
        functools.partial(gather_kernel, nx, ny, radius, cols_x, rows_y),
        out_shape=(jax.ShapeDtypeStruct((2, nx, ny, PER, members), BF), jax.ShapeDtypeStruct((nx, 8, members), F32),
                   jax.ShapeDtypeStruct((4, 2 * nx, members), F32), jax.ShapeDtypeStruct((tiles, 128, count), F32)),
        in_specs=[hbm] + [vm] * 6,
        out_specs=(hbm, vm, vm, hbm),
        scratch_shapes=[
            pltpu.VMEM(spread.shape, BF),
            pltpu.VMEM((3, PER, members), BF),
            pltpu.VMEM((8, members), F32),
            pltpu.VMEM((3, ny, PER, members), BF),
            pltpu.VMEM((8, members), F32),
            pltpu.VMEM((nx, 2, ny, PER, members), BF),
            pltpu.VMEM((nx, 8, members), F32),
            pltpu.VMEM((2, cols_x, count), F32),
            pltpu.VMEM((count, members), F32),
            pltpu.VMEM((count, members), F32),
            pltpu.VMEM((tiles, 128, count), F32),
            dma, dma((2,)), dma, dma((ny,)), dma((ny,)), dma((nx,)), dma((nx,)), dma((nx,)), dma((nx,)),
        ],
        compiler_params=pltpu.CompilerParams(collective_id=0, has_side_effects=True, vmem_limit_bytes=60 << 20),
    )(spread, mean, col, row, lev, var, val)


def chain(zx, zt, qx, dcol, ivcol, z_f32, ivar_row):
    count, members = z_f32.shape
    dof = members - 1.0
    lane = lax.broadcasted_iota(jnp.int32, (count, members), 1)
    d1, d2, d3 = split3(dcol[...])
    zx[:, :members] = z_f32.astype(BF)
    zx[:, members:] = jnp.where(lane == 0, d1.astype(F32), jnp.where(
        lane == 1, d2.astype(F32), jnp.where(lane == 2, d3.astype(F32), 0.0))).astype(BF)
    z_t = z_f32.T
    zt[...] = z_t.astype(BF)
    h1, h2, h3 = split3(z_t * (ivar_row * (1.0 / dof)))
    rhs = zx[...]
    full = mm(jnp.concatenate([h1, h2, h3], axis=0), rhs)
    full = full[:members] + full[members:2 * members] + full[2 * members:]
    row_i = lax.broadcasted_iota(jnp.int32, (members, members), 0)
    col_i = lax.broadcasted_iota(jnp.int32, (members, members), 1)
    eye = jnp.where(row_i == col_i, 1.0, 0.0).astype(F32)
    gram = full[:, :members] + eye
    vec = jnp.broadcast_to(jnp.sum(full[:, members:], axis=1, keepdims=True), (members, members))
    top = jnp.max(jnp.sum(jnp.abs(gram), axis=1, keepdims=True))
    scale = 2.0 / (1.0 + top)
    first = scale * (2.0 * eye - scale * gram)

    def more(state):
        step, miss, _ = state
        return jnp.logical_and(step < 60, miss > 1e-3)

    def newton(state):
        step, _, x = state
        resid = eye - exact(gram, x)
        x = x + exact(x, resid)
        return step + 1, jnp.max(jnp.abs(resid)), x

    _, _, inv = lax.while_loop(more, newton, (jnp.int32(0), jnp.float32(1.0), first))
    w = exact(inv, vec)
    r1, r2, r3 = split3(jnp.concatenate([inv, -w], axis=1))
    row_e = lax.broadcasted_iota(jnp.int32, (members, 2 * members), 0)
    col_e = lax.broadcasted_iota(jnp.int32, (members, 2 * members), 1)
    ones = jnp.where(jnp.logical_and(row_e < 3, col_e >= members), 1.0, 0.0).astype(BF)
    z_b = rhs[:, :members]
    acc = mm(rhs, jnp.concatenate([r1, ones], axis=0)) + mm(
        jnp.concatenate([z_b, z_b], axis=1), jnp.concatenate([r2, r3], axis=0))
    iv = ivcol[...]
    qx[...] = (acc * jnp.concatenate([iv, iv], axis=1)).astype(BF)


def update_kernel(nx, ny, step_y, spread_hbm, mean_ref, z_ref, p_ref, meta_ref, tap_hbm, mean_out, spread_out,
                  spread_in, zx, zt, qx, zf, z1, dcol, ivcol, macc, gain, tap, tap_sem, in_sem):
    levels, rows_y, cols_x, members = spread_out.shape
    count = z1.shape[0]
    loads = [pltpu.make_async_copy(tap_hbm.at[0:nx], tap.at[0:nx], tap_sem.at[0])]
    for b in range(2):
        cut = slice(nx + b * rows_y, nx + (b + 1) * rows_y)
        loads.append(pltpu.make_async_copy(tap_hbm.at[cut], tap.at[cut], tap_sem.at[b + 1]))
    fetch = pltpu.make_async_copy(spread_hbm, spread_in, in_sem)
    loads[0].start()
    fetch.start()
    loads[1].start()
    loads[2].start()

    def panel(b):
        zf[...] = z_ref[b].astype(F32).reshape(count, members)
        group = ny * PER
        return jnp.concatenate([zf[pl.ds(i * group + s, ny, stride=PER), :]
                                for i in range(nx) for s in range(PER)], axis=0)

    def rows8(q, b):
        return meta_ref[q, b * nx:(b + 1) * nx, :]

    def gap(b):
        return rows8(3, b) - jnp.concatenate([p_ref[i, b:b + 1, :] for i in range(nx)], axis=0)

    columns(gap(0), dcol)
    columns(1.0 / rows8(2, 0), ivcol)
    chain(zx, zt.at[0], qx.at[0], dcol, ivcol, panel(0), wide(1.0 / rows8(2, 0)))
    columns(gap(1), dcol)
    columns(1.0 / rows8(2, 1), ivcol)
    z1[...] = panel(1).astype(BF)
    loads[0].wait()

    def cross(c, carry):
        r = pl.ds(pl.multiple_of(c * 256, 256), 256)
        z_c = z1[r, :]
        for i in range(count // 256):
            cut = slice(i * 256, (i + 1) * 256)
            cov = mm(z_c, zt[0, :, cut])
            gain[0:256, cut] = (tap[pl.ds(2 * c, 2), :, cut].reshape(256, 256) * cov).astype(BF)
        inc = mm(gain[0:256, :], qx[0])
        z1[r, :] = (z_c.astype(F32) - 0.5 * inc[:, :members]).astype(BF)
        dcol[r, :] = dcol[r, :] - inc[:, members:]
        return carry

    lax.fori_loop(0, count // 256, cross, 0)
    chain(zx, zt.at[1], qx.at[1], dcol, ivcol, z1[...].astype(F32), wide(1.0 / rows8(2, 1)))

    macc[...] = jnp.zeros_like(macc)
    lane = lax.broadcasted_iota(jnp.int32, (cols_x, members), 1)
    fetch.wait()
    part = step_y * cols_x

    for b in range(2):
        loads[b + 1].wait()
        src = spread_in if b == 0 else spread_out

        def sweep(g, carry):
            y = g * step_y
            s = src[:, pl.ds(y, step_y)].reshape(levels * part, members)
            for i in range(count // 256):
                cut = slice(i * 256, (i + 1) * 256)
                cov = mm(s, zt[b, :, cut])
                t = tap[pl.ds(nx + b * rows_y + y, step_y), :, cut].reshape(part, 256)
                for lev in range(levels):
                    gain[lev * part:(lev + 1) * part, cut] = (t * cov[lev * part:(lev + 1) * part]).astype(BF)
            inc = mm(gain[...], qx[b])
            new = (s.astype(F32) - 0.5 * inc[:, :members]).astype(BF)
            spread_out[:, pl.ds(y, step_y)] = new.reshape(levels, step_y, cols_x, members)
            acc = macc[...]
            for lev in range(levels):
                for k in range(step_y):
                    at = (lev * step_y + k) * cols_x
                    acc = acc + jnp.where(lane == lev * rows_y + y + k, inc[at:at + cols_x, members:], 0.0)
            macc[...] = acc
            return carry

        lax.fori_loop(0, rows_y // step_y, sweep, 0)
    mean_out[...] = mean_ref[...] + macc[...].T[:levels * rows_y, :]


def update(nx, ny, step_y, spread, mean, z, p, meta, tap):
    levels, rows_y, cols_x, members = spread.shape
    count = tap.shape[2]
    vm = pl.BlockSpec(memory_space=pltpu.VMEM)
    hbm = pl.BlockSpec(memory_space=pl.ANY)
    return pl.pallas_call(
        functools.partial(update_kernel, nx, ny, step_y),
        out_shape=(jax.ShapeDtypeStruct(mean.shape, F32), jax.ShapeDtypeStruct(spread.shape, BF)),
        in_specs=[hbm, vm, vm, vm, vm, hbm],
        out_specs=(vm, vm),
        scratch_shapes=[
            pltpu.VMEM(spread.shape, BF),
            pltpu.VMEM((count, 2 * members), BF),
            pltpu.VMEM((2, members, count), BF),
            pltpu.VMEM((2, count, 2 * members), BF),
            pltpu.VMEM((count, members), F32),
            pltpu.VMEM((count, members), BF),
            pltpu.VMEM((count, members), F32),
            pltpu.VMEM((count, members), F32),
            pltpu.VMEM((cols_x, members), F32),
            pltpu.VMEM((levels * step_y * cols_x, count), BF),
            pltpu.VMEM(tap.shape, F32),
            pltpu.SemaphoreType.DMA((3,)),
            pltpu.SemaphoreType.DMA,
        ],
        compiler_params=pltpu.CompilerParams(vmem_limit_bytes=60 << 20),
    )(spread, mean, z, p, meta, tap)


def body(state_mean, state_spread, obs_value, obs_var, obs_col, obs_row, obs_level):
    levels, rows_y, cols_x, members = state_spread.shape
    nx, ny = lax.axis_size("gx"), lax.axis_size("gy")
    radius = nx * cols_x // 2
    spread = state_spread.reshape(levels * rows_y * cols_x, members)
    mean = state_mean.reshape(levels * rows_y, cols_x)

    def turn(a):
        return jnp.transpose(a, (0, 1, 3, 2)).reshape(2 * nx, PER, ny)

    z, p, meta, tap = gather(nx, ny, radius, cols_x, rows_y, spread, mean, turn(obs_col), turn(obs_row),
                             turn(obs_level), turn(obs_var), turn(obs_value))
    new_mean, new_spread = update(nx, ny, 2, state_spread, mean, z, p, meta, tap)
    return new_mean.reshape(state_mean.shape), new_spread


def solution(mesh):
    return jax.shard_map(
        body,
        mesh=mesh,
        in_specs=(P(None, "gy", "gx"), P(None, "gy", "gx", None), P(), P(), P(), P(), P()),
        out_specs=(P(None, "gy", "gx"), P(None, "gy", "gx", None)),
        check_vma=False,
    )
```

```python
import functools
import jax
import jax.numpy as jnp
from jax import lax
from jax.experimental import pallas as pl
from jax.experimental.pallas import tpu as pltpu
from jax.sharding import PartitionSpec as P

MESH = pl.DeviceIdType.MESH
HI = lax.Precision.HIGHEST
BF = jnp.bfloat16
F32 = jnp.float32
DOUBLINGS = 3
STEP_Y = 4
PER = 4
SPLIT = (6, 6)


def mm(a, b):
    return jnp.dot(a, b, preferred_element_type=F32)


def exact(a, b):
    return jnp.dot(a, b, precision=HI, preferred_element_type=F32)


def split3(x):
    a = x.astype(BF)
    r = x - a.astype(F32)
    b = r.astype(BF)
    return a, b, (r - b.astype(F32)).astype(BF)


def taper_scale(members):
    return (0.25 / (members - 1.0)) ** 0.2


def taper(sq, lam):
    rs = lax.rsqrt(sq)
    r = sq * rs
    inner = (((r - 2.0 * lam) * r - 2.5 * lam ** 2) * r + 20.0 / 3.0 * lam ** 3) * sq - 4.0 * lam ** 5
    m = jnp.maximum(2.0 * lam - r, 0.0)
    m = m * m
    m = m * m
    outer = m * (rs * (lam ** 2 / 6.0) - (r * (1.0 / 3.0) + 2.0 / 3.0 * lam))
    return jnp.minimum(inner, outer)


def columns(rows8, out):
    turned = jnp.broadcast_to(rows8[:, None, :], (8, 16, 128)).reshape(128, 128).T
    for i in range(8):
        out[i * 128:(i + 1) * 128, :] = jnp.broadcast_to(turned[:, 16 * i:16 * i + 1], (128, 128))


def wide(rows8):
    return jnp.concatenate([rows8[i:i + 1, :] for i in range(8)], axis=1)


def gather_kernel(nx, ny, radius, cols_x, rows_y, spread_hbm, mean_hbm, col_hbm, row_hbm, lev_hbm, var_hbm, val_hbm,
                  z_ref, p_ref, meta_ref, tap_ref, cells, mean_ref,
                  col_ref, row_ref, lev_ref, var_ref, val_ref, send, rows, near, pnear, allz, allp, dx2, xcol, ycol,
                  load_sem, self_sem, send_sem, recv_sem, zsend, zrecv, psend, precv):
    ax = lax.axis_index("gx")
    ay = lax.axis_index("gy")
    pairs = ((col_hbm, col_ref), (row_hbm, row_ref), (lev_hbm, lev_ref), (mean_hbm, mean_ref),
             (spread_hbm, cells), (var_hbm, var_ref), (val_hbm, val_ref))
    loads = [pltpu.make_async_copy(src, dst, load_sem.at[n]) for n, (src, dst) in enumerate(pairs)]
    for load in loads:
        load.start()
    other = ax + 1 - 2 * lax.rem(ax, 2)
    barrier = pltpu.get_barrier_semaphore()

    def greet(o, carry):
        pl.semaphore_signal(barrier, inc=1, device_id=(ax, lax.rem(ay + o, ny)), device_id_type=MESH)
        return carry

    lax.fori_loop(1, ny, greet, 0)

    def greet_x(o, carry):
        pl.semaphore_signal(barrier, inc=1, device_id=(lax.rem(ax + o, nx), ay), device_id_type=MESH)
        return carry

    lax.fori_loop(1, nx, greet_x, 0)

    members = cells.shape[1]
    total = cells.shape[0]
    lane = lax.broadcasted_iota(jnp.int32, (1, members), 1)
    place = (lax.broadcasted_iota(jnp.int32, mean_ref.shape, 0) * cols_x
             + lax.broadcasted_iota(jnp.int32, mean_ref.shape, 1)).astype(F32)

    for load in loads[:4]:
        load.wait()
    mine = []
    for b in range(2):
        at = b * nx + ax
        flat = (lev_ref[at] * rows_y + row_ref[at]) * cols_x + col_ref[at]
        pick = lax.broadcasted_iota(jnp.int32, flat.shape, 1) == ay
        mine.append(jnp.sum(jnp.where(pick, flat.astype(F32), 0.0), axis=1, keepdims=True))
    mine = jnp.concatenate(mine, axis=0)
    ids = lax.broadcasted_iota(jnp.int32, (2 * PER, total), 1).astype(F32)
    hot = jnp.where(ids == mine, 1.0, 0.0).astype(BF)
    prior = []
    for b in range(2):
        prow = jnp.zeros((1, members), F32)
        for s in range(PER):
            f = mine[b * PER + s:b * PER + s + 1, :]
            v = jnp.where(place == f, mean_ref[...], 0.0)
            v = jnp.sum(jnp.sum(v, axis=0, keepdims=True), axis=1, keepdims=True)
            prow = prow + jnp.where(lane == ny * s + ay, jnp.broadcast_to(v, (1, members)), 0.0)
        prior.append(prow)
    for b in range(2):
        hi = prior[b].astype(BF).astype(F32)
        rows[2 * b:2 * b + 1, :] = hi
        rows[2 * b + 1:2 * b + 2, :] = prior[b] - hi
    send[2] = rows[0:4, :].astype(BF)
    loads[4].wait()
    rows[...] = mm(hot, cells[...])
    send[0] = rows[0:4, :].astype(BF)
    send[1] = rows[4:8, :].astype(BF)

    pl.semaphore_wait(barrier, ny - 1 + nx - 1)

    own = pltpu.make_async_copy(send, near.at[:, ay], self_sem.at[0])
    own.start()

    def spread_out(o, carry):
        to = lax.rem(ay + o, ny)
        pltpu.make_async_remote_copy(
            send, near.at[:, ay], send_sem.at[to], recv_sem.at[ay],
            device_id=(ax, to), device_id_type=MESH).start()
        return carry

    lax.fori_loop(1, ny, spread_out, 0)
    loads[5].wait()
    loads[6].wait()

    def flatten(ref, bias):
        acc = jnp.zeros((2 * nx, members), F32)
        for s in range(PER):
            spot = jnp.where(lax.broadcasted_iota(jnp.int32, (ny, members), 1)
                             == lax.broadcasted_iota(jnp.int32, (ny, members), 0) + ny * s, 1.0, 0.0)
            acc = acc + exact(ref[:, s, :].astype(F32), spot.astype(F32))
        return acc + bias

    group = lax.rem(lax.broadcasted_iota(jnp.int32, (2 * nx, members), 0), nx)
    strip = lax.rem(lax.broadcasted_iota(jnp.int32, (2 * nx, members), 1), ny)
    meta_ref[0] = flatten(col_ref, (group * cols_x).astype(F32))
    meta_ref[1] = flatten(row_ref, (strip * rows_y).astype(F32))
    meta_ref[2] = flatten(var_ref, 0.0)
    meta_ref[3] = flatten(val_ref, 0.0)

    lam = taper_scale(members)
    inv_sq = (lam / radius) ** 2
    col_x = (ax * cols_x + lax.broadcasted_iota(jnp.int32, (cols_x, 1), 0)).astype(F32)
    ddx = col_x - wide(meta_ref[0, 0:nx, :])
    dx2[...] = ddx * ddx * inv_sq + 1e-30
    columns(meta_ref[0, nx:2 * nx, :], xcol)
    columns(meta_ref[1, nx:2 * nx, :], ycol)

    def cross_tile(i, carry):
        r = pl.ds(pl.multiple_of(i * 128, 128), 128)
        x_c, y_c = xcol[r, :], ycol[r, :]
        for c in range(nx):
            ddx = x_c - meta_ref[0, c:c + 1, :]
            ddy = y_c - meta_ref[1, c:c + 1, :]
            t = (ddx * ddx + ddy * ddy) * inv_sq + 1e-30
            tap_ref[i, :, c * 128:(c + 1) * 128] = taper(t, lam)
        return carry

    def own_tile(n, carry):
        here = (ay * rows_y + n).astype(F32)
        for c in range(nx):
            ddy = here - meta_ref[1, c:c + 1, :]
            t = dx2[:, c * 128:(c + 1) * 128] + ddy * ddy * inv_sq
            tap_ref[nx + n, :, c * 128:(c + 1) * 128] = taper(t, lam)
        return carry

    first, second = SPLIT
    lax.fori_loop(0, nx, cross_tile, 0)
    lax.fori_loop(0, first, own_tile, 0)
    own.wait()

    def arrive(o, carry):
        frm = lax.rem(ay + o, ny)
        pltpu.make_async_remote_copy(
            send, near.at[:, frm], send_sem.at[frm], recv_sem.at[frm],
            device_id=(ax, frm), device_id_type=MESH).wait()
        return carry

    lax.fori_loop(1, ny, arrive, 0)

    keep = pltpu.make_async_copy(near.at[0:2], allz.at[ax], self_sem.at[1])
    keep.start()

    def zout(o, carry):
        to = lax.rem(ax + 2 * o, nx)
        pltpu.make_async_remote_copy(near.at[0:2], allz.at[ax], zsend.at[to], zrecv.at[ax],
                                     device_id=(to, ay), device_id_type=MESH).start()
        return carry

    lax.fori_loop(1, nx // 2, zout, 0)
    pltpu.make_async_remote_copy(near.at[0:2], allz.at[ax], zsend.at[other], zrecv.at[ax],
                                 device_id=(other, ay), device_id_type=MESH).start()
    psum = jnp.sum(near[2].astype(F32), axis=0)
    pnear[0:1, :] = psum[0:1, :] + psum[1:2, :]
    pnear[1:2, :] = psum[2:3, :] + psum[3:4, :]
    allp[ax] = pnear[...]

    def pout(o, carry):
        to = lax.rem(ax + o, nx)
        pltpu.make_async_remote_copy(pnear, allp.at[ax], psend.at[to], precv.at[ax],
                                     device_id=(to, ay), device_id_type=MESH).start()
        return carry

    lax.fori_loop(1, nx, pout, 0)
    lax.fori_loop(first, first + second, own_tile, 0)

    def relay(o, carry):
        g = lax.rem(ax + 2 * o, nx)
        h = g + 1 - 2 * lax.rem(g, 2)
        pltpu.make_async_remote_copy(near.at[0:2], allz.at[g], zsend.at[g], zrecv.at[g],
                                     device_id=(g, ay), device_id_type=MESH).wait()
        pltpu.make_async_remote_copy(allz.at[g], allz.at[g], zsend.at[h], zrecv.at[g],
                                     device_id=(other, ay), device_id_type=MESH).start()
        return carry

    lax.fori_loop(1, nx // 2, relay, 0)
    lax.fori_loop(first + second, rows_y, own_tile, 0)

    def settle(o, carry):
        g = lax.rem(ax + 2 * o, nx)
        h = g + 1 - 2 * lax.rem(g, 2)
        pltpu.make_async_remote_copy(allz.at[h], allz.at[h], zsend.at[h], zrecv.at[h],
                                     device_id=(other, ay), device_id_type=MESH).wait()
        return carry

    lax.fori_loop(0, nx // 2, settle, 0)

    def settle_p(o, carry):
        g = lax.rem(ax + o, nx)
        pltpu.make_async_remote_copy(pnear, allp.at[g], psend.at[g], precv.at[g],
                                     device_id=(g, ay), device_id_type=MESH).wait()
        return carry

    lax.fori_loop(1, nx, settle_p, 0)
    keep.wait()
    p_ref[...] = allp[...]
    for b in range(2):
        z_ref[b] = allz[:, b]


def gather(nx, ny, radius, cols_x, rows_y, spread, mean, col, row, lev, var, val):
    members = spread.shape[1]
    count = nx * ny * PER
    tiles = nx + rows_y
    vm = pl.BlockSpec(memory_space=pltpu.VMEM)
    hbm = pl.BlockSpec(memory_space=pltpu.HBM)
    dma = pltpu.SemaphoreType.DMA
    return pl.pallas_call(
        functools.partial(gather_kernel, nx, ny, radius, cols_x, rows_y),
        out_shape=(pltpu.VMEM((2, nx, ny, PER, members), BF), pltpu.VMEM((nx, 8, members), F32),
                   pltpu.VMEM((4, 2 * nx, members), F32), pltpu.VMEM((tiles, 128, count), F32),
                   pltpu.VMEM(spread.shape, BF), pltpu.VMEM(mean.shape, F32)),
        in_specs=[hbm] * 7,
        out_specs=(vm,) * 6,
        scratch_shapes=[
            pltpu.VMEM(col.shape, jnp.int32),
            pltpu.VMEM(col.shape, jnp.int32),
            pltpu.VMEM(col.shape, jnp.int32),
            pltpu.VMEM(col.shape, F32),
            pltpu.VMEM(col.shape, F32),
            pltpu.VMEM((3, PER, members), BF),
            pltpu.VMEM((8, members), F32),
            pltpu.VMEM((3, ny, PER, members), BF),
            pltpu.VMEM((8, members), F32),
            pltpu.VMEM((nx, 2, ny, PER, members), BF),
            pltpu.VMEM((nx, 8, members), F32),
            pltpu.VMEM((cols_x, count), F32),
            pltpu.VMEM((count, members), F32),
            pltpu.VMEM((count, members), F32),
            dma((7,)), dma((2,)), dma((ny,)), dma((ny,)), dma((nx,)), dma((nx,)), dma((nx,)), dma((nx,)),
        ],
        compiler_params=pltpu.CompilerParams(collective_id=0, has_side_effects=True, vmem_limit_bytes=20 << 20),
    )(*[pltpu.with_memory_space_constraint(a, pltpu.HBM) for a in (spread, mean, col, row, lev, var, val)])


def chain(zx, zt, qx, dcol, ivcol, z_f32, ivar_row):
    count, members = z_f32.shape
    dof = members - 1.0
    lane = lax.broadcasted_iota(jnp.int32, (count, members), 1)
    d1, d2, d3 = split3(dcol[...])
    zx[:, :members] = z_f32.astype(BF)
    zx[:, members:] = jnp.where(lane == 0, d1.astype(F32), jnp.where(
        lane == 1, d2.astype(F32), jnp.where(lane == 2, d3.astype(F32), 0.0))).astype(BF)
    z_t = z_f32.T
    zt[...] = z_t.astype(BF)
    h1, h2, h3 = split3(z_t * (ivar_row * (1.0 / dof)))
    rhs = zx[...]
    full = mm(jnp.concatenate([h1, h2, h3], axis=0), rhs)
    full = full[:members] + full[members:2 * members] + full[2 * members:]
    row_i = lax.broadcasted_iota(jnp.int32, (members, members), 0)
    col_i = lax.broadcasted_iota(jnp.int32, (members, members), 1)
    eye = jnp.where(row_i == col_i, 1.0, 0.0).astype(F32)
    gram = full[:, :members] + eye
    vec = jnp.broadcast_to(jnp.sum(full[:, members:], axis=1, keepdims=True), (members, members))

    square = exact(gram, gram)
    top = jnp.sqrt(jnp.max(jnp.sum(jnp.abs(square), axis=1, keepdims=True), axis=0, keepdims=True))
    scale = 2.0 / (1.0 + top)
    resid = eye - 2.0 * scale * gram + scale * scale * square
    inv = scale * (2.0 * eye - scale * gram)
    for _ in range(DOUBLINGS):
        both = exact(jnp.concatenate([inv, resid], axis=0), resid)
        inv = inv + both[:members]
        resid = both[members:]
    inv = inv + exact(inv, resid)

    def more(state):
        step, miss, _ = state
        return jnp.logical_and(step < 60, miss > 1e-2)

    def newton(state):
        step, _, x = state
        resid = eye - exact(gram, x)
        x = x + exact(x, resid)
        return step + 1, jnp.max(jnp.sum(jnp.abs(resid), axis=1, keepdims=True)), x

    _, _, inv = lax.while_loop(more, newton, (jnp.int32(0), jnp.float32(1.0), inv))
    w = exact(inv, vec)
    r1, r2, r3 = split3(jnp.concatenate([inv, -w], axis=1))
    row_e = lax.broadcasted_iota(jnp.int32, (members, 2 * members), 0)
    col_e = lax.broadcasted_iota(jnp.int32, (members, 2 * members), 1)
    ones = jnp.where(jnp.logical_and(row_e < 3, col_e >= members), 1.0, 0.0).astype(BF)
    z_b = rhs[:, :members]
    acc = mm(rhs, jnp.concatenate([r1, ones], axis=0)) + mm(
        jnp.concatenate([z_b, z_b], axis=1), jnp.concatenate([r2, r3], axis=0))
    iv = ivcol[...]
    qx[...] = (acc * jnp.concatenate([iv, iv], axis=1)).astype(BF)


def update_kernel(nx, ny, radius, step_y, spread_ref, mean_ref, z_ref, p_ref, meta_ref, tap, mean_out, spread_hbm,
                  spread_out, out_sem, zx, zt, qx, zf, z1, dcol, ivcol, macc, gain, dx2, ahead):
    levels, rows_y, cols_x, members = spread_out.shape
    count = z1.shape[0]
    unit = -1.0

    def panel(b):
        zf[...] = z_ref[b].astype(F32).reshape(count, members)
        group = ny * PER
        return jnp.concatenate([zf[pl.ds(i * group + s, ny, stride=PER), :]
                                for i in range(nx) for s in range(PER)], axis=0)

    def rows8(q, b):
        return meta_ref[q, b * nx:(b + 1) * nx, :]

    def gap(b):
        return rows8(3, b) - jnp.concatenate([p_ref[i, b:b + 1, :] for i in range(nx)], axis=0)

    columns(gap(0), dcol)
    columns(1.0 / rows8(2, 0), ivcol)
    chain(zx, zt.at[0], qx.at[0], dcol, ivcol, panel(0), wide(1.0 / rows8(2, 0)))
    columns(gap(1), dcol)
    columns(1.0 / rows8(2, 1), ivcol)
    z1[...] = panel(1).astype(BF)

    def cross(c, carry):
        r = pl.ds(pl.multiple_of(c * 512, 512), 512)
        z_c = z1[r, :]
        for i in range(count // 256):
            cut = slice(i * 256, (i + 1) * 256)
            cov = mm(z_c, zt[0, :, cut])
            gain[0:512, cut] = (tap[pl.ds(4 * c, 4), :, cut].reshape(512, 256) * cov).astype(BF)
        inc = mm(gain[0:512, :], qx[0])
        z1[r, :] = (z_c.astype(F32) - (0.5 * unit) * inc[:, :members]).astype(BF)
        dcol[r, :] = dcol[r, :] - unit * inc[:, members:]
        return carry

    lax.fori_loop(0, count // 512, cross, 0)
    chain(zx, zt.at[1], qx.at[1], dcol, ivcol, z1[...].astype(F32), wide(1.0 / rows8(2, 1)))

    macc[...] = jnp.zeros_like(macc)
    lane = lax.broadcasted_iota(jnp.int32, (cols_x, members), 1)
    part = step_y * cols_x
    half = step_y // 2
    lam = taper_scale(members)
    inv_sq = (lam / radius) ** 2
    col_x = (lax.axis_index("gx") * cols_x + lax.broadcasted_iota(jnp.int32, (cols_x, 1), 0)).astype(F32)
    ddx = col_x - wide(meta_ref[0, nx:2 * nx, :])
    dx2[...] = ddx * ddx * inv_sq + 1e-30
    base_y = lax.axis_index("gy") * rows_y

    def taper_rows(y, cut):
        out = []
        for c in range(cut.start // 128, cut.stop // 128):
            ddy = (base_y + y).astype(F32) - meta_ref[1, nx + c:nx + c + 1, :]
            out.append(taper(dx2[:, c * 128:(c + 1) * 128] + ddy * ddy * inv_sq, lam))
        return jnp.concatenate(out, axis=1)

    for b in range(2):
        src = spread_ref if b == 0 else spread_out

        def sweep(g, carry):
            y = g * step_y
            s = src[:, pl.ds(y, step_y)].reshape(levels * part, members)
            for i in range(count // 256):
                cut = slice(i * 256, (i + 1) * 256)
                cov = mm(s, zt[b, :, cut])
                if b == 0:
                    t = tap[pl.ds(nx + y, step_y), :, cut].reshape(part, 256)
                    for k in range(half):
                        ahead[g * half + k, :, cut] = taper_rows(y + k, cut)
                else:
                    t = jnp.concatenate([ahead[g * half + k, :, cut] for k in range(half)]
                                        + [taper_rows(y + k, cut) for k in range(half, step_y)], axis=0)
                for lev in range(levels):
                    gain[lev * part:(lev + 1) * part, cut] = (t * cov[lev * part:(lev + 1) * part]).astype(BF)
            inc = mm(gain[...], qx[b])
            new = (s.astype(F32) - (0.5 * unit) * inc[:, :members]).astype(BF)
            spread_out[:, pl.ds(y, step_y)] = new.reshape(levels, step_y, cols_x, members)
            if b == 1:
                pltpu.make_async_copy(spread_out.at[:, pl.ds(y, step_y)], spread_hbm.at[:, pl.ds(y, step_y)],
                                      out_sem).start()
            acc = macc[...]
            for lev in range(levels):
                for k in range(step_y):
                    at = (lev * step_y + k) * cols_x
                    acc = acc + jnp.where(lane == lev * rows_y + y + k, inc[at:at + cols_x, members:], 0.0)
            macc[...] = acc
            return carry

        lax.fori_loop(0, rows_y // step_y, sweep, 0)
    pltpu.make_async_copy(spread_out, spread_hbm, out_sem).wait()
    mean_out[...] = mean_ref[...] + unit * macc[...].T[:levels * rows_y, :]


def update(nx, ny, radius, step_y, spread, mean, z, p, meta, tap):
    levels, rows_y, cols_x, members = spread.shape
    count = tap.shape[2]
    vm = pl.BlockSpec(memory_space=pltpu.VMEM)
    return pl.pallas_call(
        functools.partial(update_kernel, nx, ny, radius, step_y),
        out_shape=(jax.ShapeDtypeStruct(mean.shape, F32), jax.ShapeDtypeStruct(spread.shape, BF)),
        in_specs=[vm] * 6,
        out_specs=(vm, pl.BlockSpec(memory_space=pltpu.HBM)),
        scratch_shapes=[
            pltpu.VMEM(spread.shape, BF),
            pltpu.SemaphoreType.DMA,
            pltpu.VMEM((count, 2 * members), BF),
            pltpu.VMEM((2, members, count), BF),
            pltpu.VMEM((2, count, 2 * members), BF),
            pltpu.VMEM((count, members), F32),
            pltpu.VMEM((count, members), BF),
            pltpu.VMEM((count, members), F32),
            pltpu.VMEM((count, members), F32),
            pltpu.VMEM((cols_x, members), F32),
            pltpu.VMEM((levels * step_y * cols_x, count), BF),
            pltpu.VMEM((cols_x, count), F32),
            pltpu.VMEM((rows_y // 2, cols_x, count), F32),
        ],
        compiler_params=pltpu.CompilerParams(vmem_limit_bytes=34 << 20),
    )(spread, mean, z, p, meta, tap)


def body(state_mean, state_spread, obs_value, obs_var, obs_col, obs_row, obs_level):
    levels, rows_y, cols_x, members = state_spread.shape
    nx, ny = lax.axis_size("gx"), lax.axis_size("gy")
    radius = nx * cols_x // 2
    spread = state_spread.reshape(levels * rows_y * cols_x, members)
    mean = state_mean.reshape(levels * rows_y, cols_x)

    def turn(a):
        return jnp.transpose(a, (0, 1, 3, 2)).reshape(2 * nx, PER, ny)

    z, p, meta, tap, cells, mean = gather(nx, ny, radius, cols_x, rows_y, spread, mean, turn(obs_col), turn(obs_row),
                             turn(obs_level), turn(obs_var), turn(obs_value))
    new_mean, new_spread = update(nx, ny, radius, STEP_Y, cells.reshape(state_spread.shape), mean, z, p, meta, tap)
    return new_mean.reshape(state_mean.shape), new_spread


def solution(mesh):
    return jax.shard_map(
        body,
        mesh=mesh,
        in_specs=(P(None, "gy", "gx"), P(None, "gy", "gx", None), P(), P(), P(), P(), P()),
        out_specs=(P(None, "gy", "gx"), P(None, "gy", "gx", None)),
        check_vma=False,
    )
```

```python
import functools
import jax
import jax.numpy as jnp
from jax import lax
from jax.experimental import pallas as pl
from jax.experimental.pallas import tpu as pltpu
from jax.sharding import PartitionSpec as P

MESH = pl.DeviceIdType.MESH
HI = lax.Precision.HIGHEST
BF = jnp.bfloat16
F32 = jnp.float32
DOUBLINGS = 3
STEP_Y = 2
LEAD = 2
PER = 4
SPLIT = (6, 6)


def mm(a, b):
    return jnp.dot(a, b, preferred_element_type=F32)


def exact(a, b):
    return jnp.dot(a, b, precision=HI, preferred_element_type=F32)


def split3(x):
    a = x.astype(BF)
    r = x - a.astype(F32)
    b = r.astype(BF)
    return a, b, (r - b.astype(F32)).astype(BF)


def taper_scale(members):
    return (0.25 / (members - 1.0)) ** 0.2


def taper(sq, lam):
    rs = lax.rsqrt(sq)
    r = sq * rs
    inner = (((r - 2.0 * lam) * r - 2.5 * lam ** 2) * r + 20.0 / 3.0 * lam ** 3) * sq - 4.0 * lam ** 5
    m = jnp.maximum(2.0 * lam - r, 0.0)
    m = m * m
    m = m * m
    outer = m * (rs * (lam ** 2 / 6.0) - (r * (1.0 / 3.0) + 2.0 / 3.0 * lam))
    return jnp.minimum(inner, outer)


def columns(rows8, out):
    turned = jnp.broadcast_to(rows8[:, None, :], (8, 16, 128)).reshape(128, 128).T
    for i in range(8):
        out[i * 128:(i + 1) * 128, :] = jnp.broadcast_to(turned[:, 16 * i:16 * i + 1], (128, 128))


def wide(rows8):
    return jnp.concatenate([rows8[i:i + 1, :] for i in range(8)], axis=1)


def gather_kernel(nx, ny, radius, cols_x, rows_y, spread_hbm, mean_hbm, col_hbm, row_hbm, lev_hbm, var_hbm, val_hbm,
                  z_ref, p_ref, meta_ref, tap_ref, cells, mean_ref,
                  col_ref, row_ref, lev_ref, var_ref, val_ref, send, rows, near, pnear, allz, allp, dx2, xcol, ycol,
                  load_sem, self_sem, send_sem, recv_sem, zsend, zrecv, psend, precv):
    ax = lax.axis_index("gx")
    ay = lax.axis_index("gy")
    pairs = ((col_hbm, col_ref), (row_hbm, row_ref), (lev_hbm, lev_ref), (mean_hbm, mean_ref),
             (spread_hbm, cells), (var_hbm, var_ref), (val_hbm, val_ref))
    loads = [pltpu.make_async_copy(src, dst, load_sem.at[n]) for n, (src, dst) in enumerate(pairs)]
    for load in loads:
        load.start()
    other = ax + 1 - 2 * lax.rem(ax, 2)
    barrier = pltpu.get_barrier_semaphore()

    def greet(o, carry):
        pl.semaphore_signal(barrier, inc=1, device_id=(ax, lax.rem(ay + o, ny)), device_id_type=MESH)
        return carry

    lax.fori_loop(1, ny, greet, 0)

    def greet_x(o, carry):
        pl.semaphore_signal(barrier, inc=1, device_id=(lax.rem(ax + o, nx), ay), device_id_type=MESH)
        return carry

    lax.fori_loop(1, nx, greet_x, 0)

    members = cells.shape[1]
    total = cells.shape[0]
    lane = lax.broadcasted_iota(jnp.int32, (1, members), 1)
    place = (lax.broadcasted_iota(jnp.int32, mean_ref.shape, 0) * cols_x
             + lax.broadcasted_iota(jnp.int32, mean_ref.shape, 1)).astype(F32)

    for load in loads[:4]:
        load.wait()
    mine = []
    for b in range(2):
        at = b * nx + ax
        flat = (lev_ref[at] * rows_y + row_ref[at]) * cols_x + col_ref[at]
        pick = lax.broadcasted_iota(jnp.int32, flat.shape, 1) == ay
        mine.append(jnp.sum(jnp.where(pick, flat.astype(F32), 0.0), axis=1, keepdims=True))
    mine = jnp.concatenate(mine, axis=0)
    ids = lax.broadcasted_iota(jnp.int32, (2 * PER, total), 1).astype(F32)
    hot = jnp.where(ids == mine, 1.0, 0.0).astype(BF)
    prior = []
    for b in range(2):
        prow = jnp.zeros((1, members), F32)
        for s in range(PER):
            f = mine[b * PER + s:b * PER + s + 1, :]
            v = jnp.where(place == f, mean_ref[...], 0.0)
            v = jnp.sum(jnp.sum(v, axis=0, keepdims=True), axis=1, keepdims=True)
            prow = prow + jnp.where(lane == ny * s + ay, jnp.broadcast_to(v, (1, members)), 0.0)
        prior.append(prow)
    for b in range(2):
        hi = prior[b].astype(BF).astype(F32)
        rows[2 * b:2 * b + 1, :] = hi
        rows[2 * b + 1:2 * b + 2, :] = prior[b] - hi
    send[2] = rows[0:4, :].astype(BF)
    loads[4].wait()
    rows[...] = mm(hot, cells[...])
    send[0] = rows[0:4, :].astype(BF)
    send[1] = rows[4:8, :].astype(BF)

    pl.semaphore_wait(barrier, ny - 1 + nx - 1)

    own = pltpu.make_async_copy(send, near.at[:, ay], self_sem.at[0])
    own.start()

    def spread_out(o, carry):
        to = lax.rem(ay + o, ny)
        pltpu.make_async_remote_copy(
            send, near.at[:, ay], send_sem.at[to], recv_sem.at[ay],
            device_id=(ax, to), device_id_type=MESH).start()
        return carry

    lax.fori_loop(1, ny, spread_out, 0)
    loads[5].wait()
    loads[6].wait()

    def flatten(ref, bias):
        acc = jnp.zeros((2 * nx, members), F32)
        for s in range(PER):
            spot = jnp.where(lax.broadcasted_iota(jnp.int32, (ny, members), 1)
                             == lax.broadcasted_iota(jnp.int32, (ny, members), 0) + ny * s, 1.0, 0.0)
            acc = acc + exact(ref[:, s, :].astype(F32), spot.astype(F32))
        return acc + bias

    group = lax.rem(lax.broadcasted_iota(jnp.int32, (2 * nx, members), 0), nx)
    strip = lax.rem(lax.broadcasted_iota(jnp.int32, (2 * nx, members), 1), ny)
    meta_ref[0] = flatten(col_ref, (group * cols_x).astype(F32))
    meta_ref[1] = flatten(row_ref, (strip * rows_y).astype(F32))
    meta_ref[2] = flatten(var_ref, 0.0)
    meta_ref[3] = flatten(val_ref, 0.0)

    lam = taper_scale(members)
    inv_sq = (lam / radius) ** 2
    col_x = (ax * cols_x + lax.broadcasted_iota(jnp.int32, (cols_x, 1), 0)).astype(F32)
    ddx = col_x - wide(meta_ref[0, 0:nx, :])
    dx2[...] = ddx * ddx * inv_sq + 1e-30
    columns(meta_ref[0, nx:2 * nx, :], xcol)
    columns(meta_ref[1, nx:2 * nx, :], ycol)

    def cross_tile(i, carry):
        r = pl.ds(pl.multiple_of(i * 128, 128), 128)
        x_c, y_c = xcol[r, :], ycol[r, :]
        for c in range(nx):
            ddx = x_c - meta_ref[0, c:c + 1, :]
            ddy = y_c - meta_ref[1, c:c + 1, :]
            t = (ddx * ddx + ddy * ddy) * inv_sq + 1e-30
            tap_ref[i, :, c * 128:(c + 1) * 128] = taper(t, lam)
        return carry

    def own_tile(n, carry):
        here = (ay * rows_y + n).astype(F32)
        for c in range(nx):
            ddy = here - meta_ref[1, c:c + 1, :]
            t = dx2[:, c * 128:(c + 1) * 128] + ddy * ddy * inv_sq
            tap_ref[nx + n, :, c * 128:(c + 1) * 128] = taper(t, lam)
        return carry

    first, second = SPLIT
    lax.fori_loop(0, nx, cross_tile, 0)
    lax.fori_loop(0, first, own_tile, 0)
    own.wait()

    def arrive(o, carry):
        frm = lax.rem(ay + o, ny)
        pltpu.make_async_remote_copy(
            send, near.at[:, frm], send_sem.at[frm], recv_sem.at[frm],
            device_id=(ax, frm), device_id_type=MESH).wait()
        return carry

    lax.fori_loop(1, ny, arrive, 0)

    keep = pltpu.make_async_copy(near.at[0:2], allz.at[ax], self_sem.at[1])
    keep.start()

    def zout(o, carry):
        to = lax.rem(ax + 2 * o, nx)
        pltpu.make_async_remote_copy(near.at[0:2], allz.at[ax], zsend.at[to], zrecv.at[ax],
                                     device_id=(to, ay), device_id_type=MESH).start()
        return carry

    lax.fori_loop(1, nx // 2, zout, 0)
    pltpu.make_async_remote_copy(near.at[0:2], allz.at[ax], zsend.at[other], zrecv.at[ax],
                                 device_id=(other, ay), device_id_type=MESH).start()
    psum = jnp.sum(near[2].astype(F32), axis=0)
    pnear[0:1, :] = psum[0:1, :] + psum[1:2, :]
    pnear[1:2, :] = psum[2:3, :] + psum[3:4, :]
    allp[ax] = pnear[...]

    def pout(o, carry):
        to = lax.rem(ax + o, nx)
        pltpu.make_async_remote_copy(pnear, allp.at[ax], psend.at[to], precv.at[ax],
                                     device_id=(to, ay), device_id_type=MESH).start()
        return carry

    lax.fori_loop(1, nx, pout, 0)
    lax.fori_loop(first, first + second, own_tile, 0)

    def relay(o, carry):
        g = lax.rem(ax + 2 * o, nx)
        h = g + 1 - 2 * lax.rem(g, 2)
        pltpu.make_async_remote_copy(near.at[0:2], allz.at[g], zsend.at[g], zrecv.at[g],
                                     device_id=(g, ay), device_id_type=MESH).wait()
        pltpu.make_async_remote_copy(allz.at[g], allz.at[g], zsend.at[h], zrecv.at[g],
                                     device_id=(other, ay), device_id_type=MESH).start()
        return carry

    lax.fori_loop(1, nx // 2, relay, 0)
    lax.fori_loop(first + second, rows_y, own_tile, 0)

    def settle(o, carry):
        g = lax.rem(ax + 2 * o, nx)
        h = g + 1 - 2 * lax.rem(g, 2)
        pltpu.make_async_remote_copy(allz.at[h], allz.at[h], zsend.at[h], zrecv.at[h],
                                     device_id=(other, ay), device_id_type=MESH).wait()
        return carry

    lax.fori_loop(0, nx // 2, settle, 0)

    def settle_p(o, carry):
        g = lax.rem(ax + o, nx)
        pltpu.make_async_remote_copy(pnear, allp.at[g], psend.at[g], precv.at[g],
                                     device_id=(g, ay), device_id_type=MESH).wait()
        return carry

    lax.fori_loop(1, nx, settle_p, 0)
    keep.wait()
    p_ref[...] = allp[...]
    for b in range(2):
        z_ref[b] = allz[:, b]


def gather(nx, ny, radius, cols_x, rows_y, spread, mean, col, row, lev, var, val):
    members = spread.shape[1]
    count = nx * ny * PER
    tiles = nx + rows_y
    vm = pl.BlockSpec(memory_space=pltpu.VMEM)
    hbm = pl.BlockSpec(memory_space=pltpu.HBM)
    dma = pltpu.SemaphoreType.DMA
    return pl.pallas_call(
        functools.partial(gather_kernel, nx, ny, radius, cols_x, rows_y),
        out_shape=(pltpu.VMEM((2, nx, ny, PER, members), BF), pltpu.VMEM((nx, 8, members), F32),
                   pltpu.VMEM((4, 2 * nx, members), F32), pltpu.VMEM((tiles, 128, count), F32),
                   pltpu.VMEM(spread.shape, BF), pltpu.VMEM(mean.shape, F32)),
        in_specs=[hbm] * 7,
        out_specs=(vm,) * 6,
        scratch_shapes=[
            pltpu.VMEM(col.shape, jnp.int32),
            pltpu.VMEM(col.shape, jnp.int32),
            pltpu.VMEM(col.shape, jnp.int32),
            pltpu.VMEM(col.shape, F32),
            pltpu.VMEM(col.shape, F32),
            pltpu.VMEM((3, PER, members), BF),
            pltpu.VMEM((8, members), F32),
            pltpu.VMEM((3, ny, PER, members), BF),
            pltpu.VMEM((8, members), F32),
            pltpu.VMEM((nx, 2, ny, PER, members), BF),
            pltpu.VMEM((nx, 8, members), F32),
            pltpu.VMEM((cols_x, count), F32),
            pltpu.VMEM((count, members), F32),
            pltpu.VMEM((count, members), F32),
            dma((7,)), dma((2,)), dma((ny,)), dma((ny,)), dma((nx,)), dma((nx,)), dma((nx,)), dma((nx,)),
        ],
        compiler_params=pltpu.CompilerParams(collective_id=0, has_side_effects=True, vmem_limit_bytes=20 << 20),
    )(*[pltpu.with_memory_space_constraint(a, pltpu.HBM) for a in (spread, mean, col, row, lev, var, val)])


def chain(zx, zt, qx, dcol, ivcol, z_f32, ivar_row):
    count, members = z_f32.shape
    dof = members - 1.0
    lane = lax.broadcasted_iota(jnp.int32, (count, members), 1)
    d1, d2, d3 = split3(dcol[...])
    zx[:, :members] = z_f32.astype(BF)
    zx[:, members:] = jnp.where(lane == 0, d1.astype(F32), jnp.where(
        lane == 1, d2.astype(F32), jnp.where(lane == 2, d3.astype(F32), 0.0))).astype(BF)
    z_t = z_f32.T
    zt[...] = z_t.astype(BF)
    h1, h2, h3 = split3(z_t * (ivar_row * (1.0 / dof)))
    rhs = zx[...]
    full = mm(jnp.concatenate([h1, h2, h3], axis=0), rhs)
    full = full[:members] + full[members:2 * members] + full[2 * members:]
    row_i = lax.broadcasted_iota(jnp.int32, (members, members), 0)
    col_i = lax.broadcasted_iota(jnp.int32, (members, members), 1)
    eye = jnp.where(row_i == col_i, 1.0, 0.0).astype(F32)
    gram = full[:, :members] + eye
    vec = jnp.broadcast_to(jnp.sum(full[:, members:], axis=1, keepdims=True), (members, members))

    square = exact(gram, gram)
    top = jnp.sqrt(jnp.max(jnp.sum(jnp.abs(square), axis=1, keepdims=True), axis=0, keepdims=True))
    scale = 2.0 / (1.0 + top)
    resid = eye - 2.0 * scale * gram + scale * scale * square
    inv = scale * (2.0 * eye - scale * gram)
    for _ in range(DOUBLINGS):
        both = exact(jnp.concatenate([inv, resid], axis=0), resid)
        inv = inv + both[:members]
        resid = both[members:]
    inv = inv + exact(inv, resid)

    def more(state):
        step, miss, _ = state
        return jnp.logical_and(step < 60, miss > 1e-2)

    def newton(state):
        step, _, x = state
        resid = eye - exact(gram, x)
        x = x + exact(x, resid)
        return step + 1, jnp.max(jnp.sum(jnp.abs(resid), axis=1, keepdims=True)), x

    _, _, inv = lax.while_loop(more, newton, (jnp.int32(0), jnp.float32(1.0), inv))
    w = exact(inv, vec)
    r1, r2, r3 = split3(jnp.concatenate([inv, -w], axis=1))
    row_e = lax.broadcasted_iota(jnp.int32, (members, 2 * members), 0)
    col_e = lax.broadcasted_iota(jnp.int32, (members, 2 * members), 1)
    ones = jnp.where(jnp.logical_and(row_e < 3, col_e >= members), 1.0, 0.0).astype(BF)
    z_b = rhs[:, :members]
    acc = mm(rhs, jnp.concatenate([r1, ones], axis=0)) + mm(
        jnp.concatenate([z_b, z_b], axis=1), jnp.concatenate([r2, r3], axis=0))
    iv = ivcol[...]
    qx[...] = (acc * jnp.concatenate([iv, iv], axis=1)).astype(BF)


def update_kernel(nx, ny, radius, step_y, spread_ref, mean_ref, z_ref, p_ref, meta_ref, tap, mean_out, spread_hbm,
                  spread_out, out_sem, zx, zt, qx, zf, z1, dcol, ivcol, macc, gain, dx2, ahead):
    levels, rows_y, cols_x, members = spread_out.shape
    count = z1.shape[0]
    unit = -1.0

    def panel(b):
        zf[...] = z_ref[b].astype(F32).reshape(count, members)
        group = ny * PER
        return jnp.concatenate([zf[pl.ds(i * group + s, ny, stride=PER), :]
                                for i in range(nx) for s in range(PER)], axis=0)

    def rows8(q, b):
        return meta_ref[q, b * nx:(b + 1) * nx, :]

    def gap(b):
        return rows8(3, b) - jnp.concatenate([p_ref[i, b:b + 1, :] for i in range(nx)], axis=0)

    columns(gap(0), dcol)
    columns(1.0 / rows8(2, 0), ivcol)
    chain(zx, zt.at[0], qx.at[0], dcol, ivcol, panel(0), wide(1.0 / rows8(2, 0)))
    columns(gap(1), dcol)
    columns(1.0 / rows8(2, 1), ivcol)
    z1[...] = panel(1).astype(BF)

    def cross(c, carry):
        r = pl.ds(pl.multiple_of(c * 512, 512), 512)
        z_c = z1[r, :]
        for i in range(count // 256):
            cut = slice(i * 256, (i + 1) * 256)
            cov = mm(z_c, zt[0, :, cut])
            gain[0, 0:512, cut] = (tap[pl.ds(4 * c, 4), :, cut].reshape(512, 256) * cov).astype(BF)
        inc = mm(gain[0, 0:512, :], qx[0])
        z1[r, :] = (z_c.astype(F32) - (0.5 * unit) * inc[:, :members]).astype(BF)
        dcol[r, :] = dcol[r, :] - unit * inc[:, members:]
        return carry

    lax.fori_loop(0, count // 512, cross, 0)
    chain(zx, zt.at[1], qx.at[1], dcol, ivcol, z1[...].astype(F32), wide(1.0 / rows8(2, 1)))

    macc[...] = jnp.zeros_like(macc)
    lane = lax.broadcasted_iota(jnp.int32, (cols_x, members), 1)
    part = step_y * cols_x
    lam = taper_scale(members)
    inv_sq = (lam / radius) ** 2
    col_x = (lax.axis_index("gx") * cols_x + lax.broadcasted_iota(jnp.int32, (cols_x, 1), 0)).astype(F32)
    ddx = col_x - wide(meta_ref[0, nx:2 * nx, :])
    dx2[...] = ddx * ddx * inv_sq + 1e-30
    base_y = lax.axis_index("gy") * rows_y

    def taper_rows(y, cut):
        out = []
        for c in range(cut.start // 128, cut.stop // 128):
            ddy = (base_y + y).astype(F32) - meta_ref[1, nx + c:nx + c + 1, :]
            out.append(taper(dx2[:, c * 128:(c + 1) * 128] + ddy * ddy * inv_sq, lam))
        return jnp.concatenate(out, axis=1)

    steps = rows_y // step_y

    def rows_of(n):
        return slice((n % steps) * step_y, (n % steps + 1) * step_y)

    def spread_at(n):
        ref = spread_ref if n < steps else spread_out
        return ref[:, rows_of(n)].reshape(levels * part, members)

    def fill(n):
        b, y = n // steps, (n % steps) * step_y
        slot = gain.at[n % 2]
        s = spread_at(n)
        for i in range(count // 256):
            cut = slice(i * 256, (i + 1) * 256)
            cov = mm(s, zt[b, :, cut])
            if b == 0:
                t = tap[nx + y:nx + y + step_y, :, cut].reshape(part, 256)
            else:
                t = ahead[y:y + step_y, :, cut].reshape(part, 256)
            for lev in range(levels):
                slot[lev * part:(lev + 1) * part, cut] = (t * cov[lev * part:(lev + 1) * part]).astype(BF)

    def drain(n):
        b, y = n // steps, (n % steps) * step_y
        inc = mm(gain[n % 2], qx[b])
        new = (spread_at(n).astype(F32) - (0.5 * unit) * inc[:, :members]).astype(BF)
        spread_out[:, rows_of(n)] = new.reshape(levels, step_y, cols_x, members)
        if b == 1:
            pltpu.make_async_copy(spread_out.at[:, rows_of(n)], spread_hbm.at[:, rows_of(n)], out_sem).start()
        acc = macc[...]
        for lev in range(levels):
            for k in range(step_y):
                at = (lev * step_y + k) * cols_x
                acc = acc + jnp.where(lane == lev * rows_y + y + k, inc[at:at + cols_x, members:], 0.0)
        macc[...] = acc

    def look_ahead(y):
        for i in range(count // 256):
            cut = slice(i * 256, (i + 1) * 256)
            ahead[y, :, cut] = taper_rows(jnp.int32(y), cut)

    done = 0
    for n in range(2 * steps + 1):
        if n > 0:
            drain(n - 1)
        if n < 2 * steps:
            fill(n)
        goal = min(rows_y, LEAD + (n + 1) * rows_y // (2 * steps))
        for y in range(done, goal):
            look_ahead(y)
        done = goal
    pltpu.make_async_copy(spread_out, spread_hbm, out_sem).wait()
    mean_out[...] = mean_ref[...] + unit * macc[...].T[:levels * rows_y, :]


def update(nx, ny, radius, step_y, spread, mean, z, p, meta, tap):
    levels, rows_y, cols_x, members = spread.shape
    count = tap.shape[2]
    vm = pl.BlockSpec(memory_space=pltpu.VMEM)
    return pl.pallas_call(
        functools.partial(update_kernel, nx, ny, radius, step_y),
        out_shape=(jax.ShapeDtypeStruct(mean.shape, F32), jax.ShapeDtypeStruct(spread.shape, BF)),
        in_specs=[vm] * 6,
        out_specs=(vm, pl.BlockSpec(memory_space=pltpu.HBM)),
        scratch_shapes=[
            pltpu.VMEM(spread.shape, BF),
            pltpu.SemaphoreType.DMA,
            pltpu.VMEM((count, 2 * members), BF),
            pltpu.VMEM((2, members, count), BF),
            pltpu.VMEM((2, count, 2 * members), BF),
            pltpu.VMEM((count, members), F32),
            pltpu.VMEM((count, members), BF),
            pltpu.VMEM((count, members), F32),
            pltpu.VMEM((count, members), F32),
            pltpu.VMEM((cols_x, members), F32),
            pltpu.VMEM((2, levels * step_y * cols_x, count), BF),
            pltpu.VMEM((cols_x, count), F32),
            pltpu.VMEM((rows_y, cols_x, count), F32),
        ],
        compiler_params=pltpu.CompilerParams(vmem_limit_bytes=34 << 20),
    )(spread, mean, z, p, meta, tap)


def body(state_mean, state_spread, obs_value, obs_var, obs_col, obs_row, obs_level):
    levels, rows_y, cols_x, members = state_spread.shape
    nx, ny = lax.axis_size("gx"), lax.axis_size("gy")
    radius = nx * cols_x // 2
    spread = state_spread.reshape(levels * rows_y * cols_x, members)
    mean = state_mean.reshape(levels * rows_y, cols_x)

    def turn(a):
        return jnp.transpose(a, (0, 1, 3, 2)).reshape(2 * nx, PER, ny)

    z, p, meta, tap, cells, mean = gather(nx, ny, radius, cols_x, rows_y, spread, mean, turn(obs_col), turn(obs_row),
                             turn(obs_level), turn(obs_var), turn(obs_value))
    new_mean, new_spread = update(nx, ny, radius, STEP_Y, cells.reshape(state_spread.shape), mean, z, p, meta, tap)
    return new_mean.reshape(state_mean.shape), new_spread


def solution(mesh):
    return jax.shard_map(
        body,
        mesh=mesh,
        in_specs=(P(None, "gy", "gx"), P(None, "gy", "gx", None), P(), P(), P(), P(), P()),
        out_specs=(P(None, "gy", "gx"), P(None, "gy", "gx", None)),
        check_vma=False,
    )
```

```python
import functools
import jax
import jax.numpy as jnp
from jax import lax
from jax.experimental import pallas as pl
from jax.experimental.pallas import tpu as pltpu
from jax.sharding import PartitionSpec as P

MESH = pl.DeviceIdType.MESH
HI = lax.Precision.HIGHEST
BF = jnp.bfloat16
F32 = jnp.float32
DOUBLINGS = 3
STEP_Y = 2
LEAD = 2
PER = 4
SPLIT = (4, 6)


def mm(a, b):
    return jnp.dot(a, b, preferred_element_type=F32)


def exact(a, b):
    return jnp.dot(a, b, precision=HI, preferred_element_type=F32)


def mm3(a, b):
    a1 = a.astype(BF)
    a2 = (a - a1.astype(F32)).astype(BF)
    b1 = b.astype(BF)
    b2 = (b - b1.astype(F32)).astype(BF)
    return mm(jnp.concatenate([a1, a2], axis=1), jnp.concatenate([b1, b1], axis=0)) + mm(a1, b2)


def split3(x):
    a = x.astype(BF)
    r = x - a.astype(F32)
    b = r.astype(BF)
    return a, b, (r - b.astype(F32)).astype(BF)


def taper_scale(members):
    return (0.25 / (members - 1.0)) ** 0.2


def taper(sq, lam):
    rs = lax.rsqrt(sq)
    r = sq * rs
    inner = (((r - 2.0 * lam) * r - 2.5 * lam ** 2) * r + 20.0 / 3.0 * lam ** 3) * sq - 4.0 * lam ** 5
    m = jnp.maximum(2.0 * lam - r, 0.0)
    m = m * m
    m = m * m
    outer = m * (rs * (lam ** 2 / 6.0) - (r * (1.0 / 3.0) + 2.0 / 3.0 * lam))
    return jnp.minimum(inner, outer)


def columns(rows8, out):
    turned = jnp.broadcast_to(rows8[:, None, :], (8, 16, 128)).reshape(128, 128).T
    for i in range(8):
        out[i * 128:(i + 1) * 128, :] = jnp.broadcast_to(turned[:, 16 * i:16 * i + 1], (128, 128))


def wide(rows8):
    return jnp.concatenate([rows8[i:i + 1, :] for i in range(8)], axis=1)


def gather_kernel(nx, ny, radius, cols_x, rows_y, spread_hbm, mean_hbm, col_hbm, row_hbm, lev_hbm, var_hbm, val_hbm,
                  z_ref, p_ref, meta_ref, tap_ref, cells, mean_ref,
                  col_ref, row_ref, lev_ref, var_ref, val_ref, send, rows, near, pnear, allz, allp, dx2, xcol, ycol,
                  load_sem, self_sem, send_sem, recv_sem, zsend, zrecv, psend, precv):
    ax = lax.axis_index("gx")
    ay = lax.axis_index("gy")
    pairs = ((col_hbm, col_ref), (row_hbm, row_ref), (lev_hbm, lev_ref), (mean_hbm, mean_ref),
             (spread_hbm, cells), (var_hbm, var_ref), (val_hbm, val_ref))
    loads = [pltpu.make_async_copy(src, dst, load_sem.at[n]) for n, (src, dst) in enumerate(pairs)]
    for load in loads:
        load.start()
    other = ax + 1 - 2 * lax.rem(ax, 2)
    barrier = pltpu.get_barrier_semaphore()

    def greet(o, carry):
        pl.semaphore_signal(barrier, inc=1, device_id=(ax, lax.rem(ay + o, ny)), device_id_type=MESH)
        return carry

    lax.fori_loop(1, ny, greet, 0)

    def greet_x(o, carry):
        pl.semaphore_signal(barrier, inc=1, device_id=(lax.rem(ax + o, nx), ay), device_id_type=MESH)
        return carry

    lax.fori_loop(1, nx, greet_x, 0)

    members = cells.shape[1]
    total = cells.shape[0]
    lane = lax.broadcasted_iota(jnp.int32, (1, members), 1)
    place = (lax.broadcasted_iota(jnp.int32, mean_ref.shape, 0) * cols_x
             + lax.broadcasted_iota(jnp.int32, mean_ref.shape, 1)).astype(F32)

    for load in loads[:4]:
        load.wait()
    mine = []
    for b in range(2):
        at = b * nx + ax
        flat = (lev_ref[at] * rows_y + row_ref[at]) * cols_x + col_ref[at]
        pick = lax.broadcasted_iota(jnp.int32, flat.shape, 1) == ay
        mine.append(jnp.sum(jnp.where(pick, flat.astype(F32), 0.0), axis=1, keepdims=True))
    mine = jnp.concatenate(mine, axis=0)
    ids = lax.broadcasted_iota(jnp.int32, (2 * PER, total), 1).astype(F32)
    hot = jnp.where(ids == mine, 1.0, 0.0).astype(BF)
    prior = []
    for b in range(2):
        prow = jnp.zeros((1, members), F32)
        for s in range(PER):
            f = mine[b * PER + s:b * PER + s + 1, :]
            v = jnp.where(place == f, mean_ref[...], 0.0)
            v = jnp.sum(jnp.sum(v, axis=0, keepdims=True), axis=1, keepdims=True)
            prow = prow + jnp.where(lane == ny * s + ay, jnp.broadcast_to(v, (1, members)), 0.0)
        prior.append(prow)
    for b in range(2):
        hi = prior[b].astype(BF).astype(F32)
        rows[2 * b:2 * b + 1, :] = hi
        rows[2 * b + 1:2 * b + 2, :] = prior[b] - hi
    send[2] = rows[0:4, :].astype(BF)
    loads[4].wait()
    rows[...] = mm(hot, cells[...])
    send[0] = rows[0:4, :].astype(BF)
    send[1] = rows[4:8, :].astype(BF)

    pl.semaphore_wait(barrier, ny - 1 + nx - 1)

    own = pltpu.make_async_copy(send, near.at[:, ay], self_sem.at[0])
    own.start()

    def spread_out(o, carry):
        to = lax.rem(ay + o, ny)
        pltpu.make_async_remote_copy(
            send, near.at[:, ay], send_sem.at[to], recv_sem.at[ay],
            device_id=(ax, to), device_id_type=MESH).start()
        return carry

    lax.fori_loop(1, ny, spread_out, 0)
    loads[5].wait()
    loads[6].wait()

    def flatten(ref, bias):
        acc = jnp.zeros((2 * nx, members), F32)
        for s in range(PER):
            spot = jnp.where(lax.broadcasted_iota(jnp.int32, (ny, members), 1)
                             == lax.broadcasted_iota(jnp.int32, (ny, members), 0) + ny * s, 1.0, 0.0)
            acc = acc + exact(ref[:, s, :].astype(F32), spot.astype(F32))
        return acc + bias

    group = lax.rem(lax.broadcasted_iota(jnp.int32, (2 * nx, members), 0), nx)
    strip = lax.rem(lax.broadcasted_iota(jnp.int32, (2 * nx, members), 1), ny)
    meta_ref[0] = flatten(col_ref, (group * cols_x).astype(F32))
    meta_ref[1] = flatten(row_ref, (strip * rows_y).astype(F32))
    meta_ref[2] = flatten(var_ref, 0.0)
    meta_ref[3] = flatten(val_ref, 0.0)

    lam = taper_scale(members)
    inv_sq = (lam / radius) ** 2
    col_x = (ax * cols_x + lax.broadcasted_iota(jnp.int32, (cols_x, 1), 0)).astype(F32)
    ddx = col_x - wide(meta_ref[0, 0:nx, :])
    dx2[...] = ddx * ddx * inv_sq + 1e-30
    columns(meta_ref[0, nx:2 * nx, :], xcol)
    columns(meta_ref[1, nx:2 * nx, :], ycol)

    def cross_tile(i, carry):
        r = pl.ds(pl.multiple_of(i * 128, 128), 128)
        x_c, y_c = xcol[r, :], ycol[r, :]
        for c in range(nx):
            ddx = x_c - meta_ref[0, c:c + 1, :]
            ddy = y_c - meta_ref[1, c:c + 1, :]
            t = (ddx * ddx + ddy * ddy) * inv_sq + 1e-30
            tap_ref[i, :, c * 128:(c + 1) * 128] = taper(t, lam)
        return carry

    def own_tile(n, carry):
        here = (ay * rows_y + n).astype(F32)
        for c in range(nx):
            ddy = here - meta_ref[1, c:c + 1, :]
            t = dx2[:, c * 128:(c + 1) * 128] + ddy * ddy * inv_sq
            tap_ref[nx + n, :, c * 128:(c + 1) * 128] = taper(t, lam)
        return carry

    first, second = SPLIT
    lax.fori_loop(0, nx, cross_tile, 0)
    lax.fori_loop(0, first, own_tile, 0)
    own.wait()

    def arrive(o, carry):
        frm = lax.rem(ay + o, ny)
        pltpu.make_async_remote_copy(
            send, near.at[:, frm], send_sem.at[frm], recv_sem.at[frm],
            device_id=(ax, frm), device_id_type=MESH).wait()
        return carry

    lax.fori_loop(1, ny, arrive, 0)

    keep = pltpu.make_async_copy(near.at[0:2], allz.at[ax], self_sem.at[1])
    keep.start()

    def zout(o, carry):
        to = lax.rem(ax + 2 * o, nx)
        pltpu.make_async_remote_copy(near.at[0:2], allz.at[ax], zsend.at[to], zrecv.at[ax],
                                     device_id=(to, ay), device_id_type=MESH).start()
        return carry

    lax.fori_loop(1, nx // 2, zout, 0)
    pltpu.make_async_remote_copy(near.at[0:2], allz.at[ax], zsend.at[other], zrecv.at[ax],
                                 device_id=(other, ay), device_id_type=MESH).start()
    psum = jnp.sum(near[2].astype(F32), axis=0)
    pnear[0:1, :] = psum[0:1, :] + psum[1:2, :]
    pnear[1:2, :] = psum[2:3, :] + psum[3:4, :]
    allp[ax] = pnear[...]

    def pout(o, carry):
        to = lax.rem(ax + o, nx)
        pltpu.make_async_remote_copy(pnear, allp.at[ax], psend.at[to], precv.at[ax],
                                     device_id=(to, ay), device_id_type=MESH).start()
        return carry

    lax.fori_loop(1, nx, pout, 0)
    lax.fori_loop(first, first + second, own_tile, 0)

    def relay(o, carry):
        g = lax.rem(ax + 2 * o, nx)
        h = g + 1 - 2 * lax.rem(g, 2)
        pltpu.make_async_remote_copy(near.at[0:2], allz.at[g], zsend.at[g], zrecv.at[g],
                                     device_id=(g, ay), device_id_type=MESH).wait()
        pltpu.make_async_remote_copy(allz.at[g], allz.at[g], zsend.at[h], zrecv.at[g],
                                     device_id=(other, ay), device_id_type=MESH).start()
        return carry

    lax.fori_loop(1, nx // 2, relay, 0)
    lax.fori_loop(first + second, rows_y, own_tile, 0)

    def settle(o, carry):
        g = lax.rem(ax + 2 * o, nx)
        h = g + 1 - 2 * lax.rem(g, 2)
        pltpu.make_async_remote_copy(allz.at[h], allz.at[h], zsend.at[h], zrecv.at[h],
                                     device_id=(other, ay), device_id_type=MESH).wait()
        return carry

    lax.fori_loop(0, nx // 2, settle, 0)

    def settle_p(o, carry):
        g = lax.rem(ax + o, nx)
        pltpu.make_async_remote_copy(pnear, allp.at[g], psend.at[g], precv.at[g],
                                     device_id=(g, ay), device_id_type=MESH).wait()
        return carry

    lax.fori_loop(1, nx, settle_p, 0)
    keep.wait()
    p_ref[...] = allp[...]
    for b in range(2):
        z_ref[b] = allz[:, b]


def gather(nx, ny, radius, cols_x, rows_y, spread, mean, col, row, lev, var, val):
    members = spread.shape[1]
    count = nx * ny * PER
    tiles = nx + rows_y
    vm = pl.BlockSpec(memory_space=pltpu.VMEM)
    hbm = pl.BlockSpec(memory_space=pltpu.HBM)
    dma = pltpu.SemaphoreType.DMA
    return pl.pallas_call(
        functools.partial(gather_kernel, nx, ny, radius, cols_x, rows_y),
        out_shape=(pltpu.VMEM((2, nx, ny, PER, members), BF), pltpu.VMEM((nx, 8, members), F32),
                   pltpu.VMEM((4, 2 * nx, members), F32), pltpu.VMEM((tiles, 128, count), F32),
                   pltpu.VMEM(spread.shape, BF), pltpu.VMEM(mean.shape, F32)),
        in_specs=[hbm] * 7,
        out_specs=(vm,) * 6,
        scratch_shapes=[
            pltpu.VMEM(col.shape, jnp.int32),
            pltpu.VMEM(col.shape, jnp.int32),
            pltpu.VMEM(col.shape, jnp.int32),
            pltpu.VMEM(col.shape, F32),
            pltpu.VMEM(col.shape, F32),
            pltpu.VMEM((3, PER, members), BF),
            pltpu.VMEM((8, members), F32),
            pltpu.VMEM((3, ny, PER, members), BF),
            pltpu.VMEM((8, members), F32),
            pltpu.VMEM((nx, 2, ny, PER, members), BF),
            pltpu.VMEM((nx, 8, members), F32),
            pltpu.VMEM((cols_x, count), F32),
            pltpu.VMEM((count, members), F32),
            pltpu.VMEM((count, members), F32),
            dma((7,)), dma((2,)), dma((ny,)), dma((ny,)), dma((nx,)), dma((nx,)), dma((nx,)), dma((nx,)),
        ],
        compiler_params=pltpu.CompilerParams(collective_id=0, has_side_effects=True, vmem_limit_bytes=20 << 20),
    )(*[pltpu.with_memory_space_constraint(a, pltpu.HBM) for a in (spread, mean, col, row, lev, var, val)])


def chain(zx, zt, dcol, z_f32, ivar_row):
    count, members = z_f32.shape
    dof = members - 1.0
    lane = lax.broadcasted_iota(jnp.int32, (count, members), 1)
    d1, d2, d3 = split3(dcol[...])
    zx[:, :members] = z_f32.astype(BF)
    zx[:, members:] = jnp.where(lane == 0, d1.astype(F32), jnp.where(
        lane == 1, d2.astype(F32), jnp.where(lane == 2, d3.astype(F32), 0.0))).astype(BF)
    z_t = z_f32.T
    zt[...] = z_t.astype(BF)
    h1, h2, h3 = split3(z_t * (ivar_row * (1.0 / dof)))
    rhs = zx[...]
    full = mm(jnp.concatenate([h1, h2, h3], axis=0), rhs)
    full = full[:members] + full[members:2 * members] + full[2 * members:]
    row_i = lax.broadcasted_iota(jnp.int32, (members, members), 0)
    col_i = lax.broadcasted_iota(jnp.int32, (members, members), 1)
    eye = jnp.where(row_i == col_i, 1.0, 0.0).astype(F32)
    gram = full[:, :members] + eye
    vec = jnp.broadcast_to(jnp.sum(full[:, members:], axis=1, keepdims=True), (members, members))

    square = exact(gram, gram)
    top = jnp.sqrt(jnp.max(jnp.sum(jnp.abs(square), axis=1, keepdims=True), axis=0, keepdims=True))
    scale = 2.0 / (1.0 + top)
    resid = eye - 2.0 * scale * gram + scale * scale * square
    inv = scale * (2.0 * eye - scale * gram)
    for _ in range(DOUBLINGS):
        both = mm3(jnp.concatenate([inv, resid], axis=0), resid)
        inv = inv + both[:members]
        resid = both[members:]
    inv = inv + mm3(inv, resid)
    return gram, vec, inv


def chain_end(zx, qx, ivcol, gram, vec, inv):
    members = gram.shape[0]
    rhs = zx[...]
    eye = jnp.where(lax.broadcasted_iota(jnp.int32, gram.shape, 0)
                    == lax.broadcasted_iota(jnp.int32, gram.shape, 1), 1.0, 0.0).astype(F32)

    def more(state):
        step, miss, _ = state
        return jnp.logical_and(step < 60, miss > 1e-2)

    def newton(state):
        step, _, x = state
        resid = eye - exact(gram, x)
        x = x + exact(x, resid)
        return step + 1, jnp.max(jnp.sum(jnp.abs(resid), axis=1, keepdims=True)), x

    _, _, inv = lax.while_loop(more, newton, (jnp.int32(0), jnp.float32(1.0), inv))
    w = exact(inv, vec)
    r1, r2, r3 = split3(jnp.concatenate([inv, -w], axis=1))
    row_e = lax.broadcasted_iota(jnp.int32, (members, 2 * members), 0)
    col_e = lax.broadcasted_iota(jnp.int32, (members, 2 * members), 1)
    ones = jnp.where(jnp.logical_and(row_e < 3, col_e >= members), 1.0, 0.0).astype(BF)
    z_b = rhs[:, :members]
    acc = mm(rhs, jnp.concatenate([r1, ones], axis=0)) + mm(
        jnp.concatenate([z_b, z_b], axis=1), jnp.concatenate([r2, r3], axis=0))
    iv = ivcol[...]
    qx[...] = (acc * jnp.concatenate([iv, iv], axis=1)).astype(BF)


def update_kernel(nx, ny, radius, step_y, spread_ref, mean_ref, z_ref, p_ref, meta_ref, tap, mean_out, spread_hbm,
                  spread_out, out_sem, zx, zt, qx, zf, z1, dcol, ivcol, macc, gain, dx2, ahead):
    levels, rows_y, cols_x, members = spread_out.shape
    count = z1.shape[0]
    unit = -1.0

    def panel(b):
        zf[...] = z_ref[b].astype(F32).reshape(count, members)
        group = ny * PER
        return jnp.concatenate([zf[pl.ds(i * group + s, ny, stride=PER), :]
                                for i in range(nx) for s in range(PER)], axis=0)

    def rows8(q, b):
        return meta_ref[q, b * nx:(b + 1) * nx, :]

    def gap(b):
        return rows8(3, b) - jnp.concatenate([p_ref[i, b:b + 1, :] for i in range(nx)], axis=0)

    columns(gap(0), dcol)
    columns(1.0 / rows8(2, 0), ivcol)
    state = chain(zx, zt.at[0], dcol, panel(0), wide(1.0 / rows8(2, 0)))
    chain_end(zx, qx.at[0], ivcol, *state)
    columns(gap(1), dcol)
    columns(1.0 / rows8(2, 1), ivcol)
    z1[...] = panel(1).astype(BF)

    def cross_fill(c):
        for i in range(count // 256):
            cut = slice(i * 256, (i + 1) * 256)
            cov = mm(z1[c * 512:(c + 1) * 512, :], zt[0, :, cut])
            gain[c % 2, 0:512, cut] = (tap[4 * c:4 * c + 4, :, cut].reshape(512, 256) * cov).astype(BF)

    def cross_drain(c):
        r = slice(c * 512, (c + 1) * 512)
        inc = mm(gain[c % 2, 0:512, :], qx[0])
        z1[r, :] = (z1[r, :].astype(F32) - (0.5 * unit) * inc[:, :members]).astype(BF)
        dcol[r, :] = dcol[r, :] - unit * inc[:, members:]

    for c in range(count // 512 + 1):
        if c > 0:
            cross_drain(c - 1)
        if c < count // 512:
            cross_fill(c)
    state = chain(zx, zt.at[1], dcol, z1[...].astype(F32), wide(1.0 / rows8(2, 1)))
    chain_end(zx, qx.at[1], ivcol, *state)

    macc[...] = jnp.zeros_like(macc)
    lane = lax.broadcasted_iota(jnp.int32, (cols_x, members), 1)
    part = step_y * cols_x
    lam = taper_scale(members)
    inv_sq = (lam / radius) ** 2
    col_x = (lax.axis_index("gx") * cols_x + lax.broadcasted_iota(jnp.int32, (cols_x, 1), 0)).astype(F32)
    ddx = col_x - wide(meta_ref[0, nx:2 * nx, :])
    dx2[...] = ddx * ddx * inv_sq + 1e-30
    base_y = lax.axis_index("gy") * rows_y

    def taper_rows(y, cut):
        out = []
        for c in range(cut.start // 128, cut.stop // 128):
            ddy = (base_y + y).astype(F32) - meta_ref[1, nx + c:nx + c + 1, :]
            out.append(taper(dx2[:, c * 128:(c + 1) * 128] + ddy * ddy * inv_sq, lam))
        return jnp.concatenate(out, axis=1)

    steps = rows_y // step_y

    def rows_of(n):
        return slice((n % steps) * step_y, (n % steps + 1) * step_y)

    def spread_at(n):
        ref = spread_ref if n < steps else spread_out
        return ref[:, rows_of(n)].reshape(levels * part, members)

    def fill(n):
        b, y = n // steps, (n % steps) * step_y
        slot = gain.at[n % 2]
        s = spread_at(n)
        for i in range(count // 256):
            cut = slice(i * 256, (i + 1) * 256)
            cov = mm(s, zt[b, :, cut])
            if b == 0:
                t = tap[nx + y:nx + y + step_y, :, cut].reshape(part, 256)
            else:
                t = ahead[y:y + step_y, :, cut].reshape(part, 256)
            for lev in range(levels):
                slot[lev * part:(lev + 1) * part, cut] = (t * cov[lev * part:(lev + 1) * part]).astype(BF)

    def drain(n):
        b, y = n // steps, (n % steps) * step_y
        inc = mm(gain[n % 2], qx[b])
        new = (spread_at(n).astype(F32) - (0.5 * unit) * inc[:, :members]).astype(BF)
        spread_out[:, rows_of(n)] = new.reshape(levels, step_y, cols_x, members)
        if b == 1:
            pltpu.make_async_copy(spread_out.at[:, rows_of(n)], spread_hbm.at[:, rows_of(n)], out_sem).start()
        acc = macc[...]
        for lev in range(levels):
            for k in range(step_y):
                at = (lev * step_y + k) * cols_x
                acc = acc + jnp.where(lane == lev * rows_y + y + k, inc[at:at + cols_x, members:], 0.0)
        macc[...] = acc

    def look_ahead(y):
        for i in range(count // 256):
            cut = slice(i * 256, (i + 1) * 256)
            ahead[y, :, cut] = taper_rows(jnp.int32(y), cut)

    done = 0
    for n in range(2 * steps + 1):
        if n > 0:
            drain(n - 1)
        if n < 2 * steps:
            fill(n)
        goal = min(rows_y, LEAD + (n + 1) * rows_y // (2 * steps))
        for y in range(done, goal):
            look_ahead(y)
        done = goal
    pltpu.make_async_copy(spread_out, spread_hbm, out_sem).wait()
    mean_out[...] = mean_ref[...] + unit * macc[...].T[:levels * rows_y, :]


def update(nx, ny, radius, step_y, spread, mean, z, p, meta, tap):
    levels, rows_y, cols_x, members = spread.shape
    count = tap.shape[2]
    vm = pl.BlockSpec(memory_space=pltpu.VMEM)
    return pl.pallas_call(
        functools.partial(update_kernel, nx, ny, radius, step_y),
        out_shape=(jax.ShapeDtypeStruct(mean.shape, F32), jax.ShapeDtypeStruct(spread.shape, BF)),
        in_specs=[vm] * 6,
        out_specs=(vm, pl.BlockSpec(memory_space=pltpu.HBM)),
        scratch_shapes=[
            pltpu.VMEM(spread.shape, BF),
            pltpu.SemaphoreType.DMA,
            pltpu.VMEM((count, 2 * members), BF),
            pltpu.VMEM((2, members, count), BF),
            pltpu.VMEM((2, count, 2 * members), BF),
            pltpu.VMEM((count, members), F32),
            pltpu.VMEM((count, members), BF),
            pltpu.VMEM((count, members), F32),
            pltpu.VMEM((count, members), F32),
            pltpu.VMEM((cols_x, members), F32),
            pltpu.VMEM((2, levels * step_y * cols_x, count), BF),
            pltpu.VMEM((cols_x, count), F32),
            pltpu.VMEM((rows_y, cols_x, count), F32),
        ],
        compiler_params=pltpu.CompilerParams(vmem_limit_bytes=34 << 20),
    )(spread, mean, z, p, meta, tap)


def body(state_mean, state_spread, obs_value, obs_var, obs_col, obs_row, obs_level):
    levels, rows_y, cols_x, members = state_spread.shape
    nx, ny = lax.axis_size("gx"), lax.axis_size("gy")
    radius = nx * cols_x // 2
    spread = state_spread.reshape(levels * rows_y * cols_x, members)
    mean = state_mean.reshape(levels * rows_y, cols_x)

    def turn(a):
        return jnp.transpose(a, (0, 1, 3, 2)).reshape(2 * nx, PER, ny)

    z, p, meta, tap, cells, mean = gather(nx, ny, radius, cols_x, rows_y, spread, mean, turn(obs_col), turn(obs_row),
                             turn(obs_level), turn(obs_var), turn(obs_value))
    new_mean, new_spread = update(nx, ny, radius, STEP_Y, cells.reshape(state_spread.shape), mean, z, p, meta, tap)
    return new_mean.reshape(state_mean.shape), new_spread


def solution(mesh):
    return jax.shard_map(
        body,
        mesh=mesh,
        in_specs=(P(None, "gy", "gx"), P(None, "gy", "gx", None), P(), P(), P(), P(), P()),
        out_specs=(P(None, "gy", "gx"), P(None, "gy", "gx", None)),
        check_vma=False,
    )
```

```python
import functools
import jax
import jax.numpy as jnp
from jax import lax
from jax.experimental import pallas as pl
from jax.experimental.pallas import tpu as pltpu
from jax.sharding import PartitionSpec as P

MESH = pl.DeviceIdType.MESH
HI = lax.Precision.HIGHEST
BF = jnp.bfloat16
F32 = jnp.float32
DOUBLINGS = 3
STEP_Y = 2
LEAD = 2
PER = 4
SPLIT = (2, 6)


def mm(a, b):
    return jnp.dot(a, b, preferred_element_type=F32)


def exact(a, b):
    return jnp.dot(a, b, precision=HI, preferred_element_type=F32)


def mm3(a, b):
    a1 = a.astype(BF)
    a2 = (a - a1.astype(F32)).astype(BF)
    b1 = b.astype(BF)
    b2 = (b - b1.astype(F32)).astype(BF)
    return mm(jnp.concatenate([a1, a2], axis=1), jnp.concatenate([b1, b1], axis=0)) + mm(a1, b2)


def split3(x):
    a = x.astype(BF)
    r = x - a.astype(F32)
    b = r.astype(BF)
    return a, b, (r - b.astype(F32)).astype(BF)


def taper_scale(members):
    return (0.25 / (members - 1.0)) ** 0.2


def taper(sq, lam):
    rs = lax.rsqrt(sq)
    r = sq * rs
    inner = (((r - 2.0 * lam) * r - 2.5 * lam ** 2) * r + 20.0 / 3.0 * lam ** 3) * sq - 4.0 * lam ** 5
    m = jnp.maximum(2.0 * lam - r, 0.0)
    m = m * m
    m = m * m
    outer = m * (rs * (lam ** 2 / 6.0) - (r * (1.0 / 3.0) + 2.0 / 3.0 * lam))
    return jnp.minimum(inner, outer)


def columns(rows8, out):
    turned = jnp.broadcast_to(rows8[:, None, :], (8, 16, 128)).reshape(128, 128).T
    for i in range(8):
        out[i * 128:(i + 1) * 128, :] = jnp.broadcast_to(turned[:, 16 * i:16 * i + 1], (128, 128))


def wide(rows8):
    return jnp.concatenate([rows8[i:i + 1, :] for i in range(8)], axis=1)


def gather_kernel(nx, ny, radius, cols_x, rows_y, spread_hbm, mean_hbm, col_hbm, row_hbm, lev_hbm, var_hbm, val_hbm,
                  z_ref, p_ref, meta_ref, tap_ref, cells, mean_ref,
                  col_ref, row_ref, lev_ref, var_ref, val_ref, send, rows, near, pnear, allz, allp, dx2, xcol, ycol,
                  load_sem, self_sem, send_sem, recv_sem, zsend, zrecv, psend, precv):
    ax = lax.axis_index("gx")
    ay = lax.axis_index("gy")
    pairs = ((col_hbm, col_ref), (row_hbm, row_ref), (lev_hbm, lev_ref), (mean_hbm, mean_ref),
             (spread_hbm, cells), (var_hbm, var_ref), (val_hbm, val_ref))
    loads = [pltpu.make_async_copy(src, dst, load_sem.at[n]) for n, (src, dst) in enumerate(pairs)]
    for load in loads:
        load.start()
    other = ax + 1 - 2 * lax.rem(ax, 2)
    barrier = pltpu.get_barrier_semaphore()

    def greet(o, carry):
        pl.semaphore_signal(barrier, inc=1, device_id=(ax, lax.rem(ay + o, ny)), device_id_type=MESH)
        return carry

    lax.fori_loop(1, ny, greet, 0)

    def greet_x(o, carry):
        pl.semaphore_signal(barrier, inc=1, device_id=(lax.rem(ax + o, nx), ay), device_id_type=MESH)
        return carry

    lax.fori_loop(1, nx, greet_x, 0)

    members = cells.shape[1]
    total = cells.shape[0]
    lane = lax.broadcasted_iota(jnp.int32, (1, members), 1)
    place = (lax.broadcasted_iota(jnp.int32, mean_ref.shape, 0) * cols_x
             + lax.broadcasted_iota(jnp.int32, mean_ref.shape, 1)).astype(F32)

    for load in loads[:4]:
        load.wait()
    mine = []
    for b in range(2):
        at = b * nx + ax
        flat = (lev_ref[at] * rows_y + row_ref[at]) * cols_x + col_ref[at]
        pick = lax.broadcasted_iota(jnp.int32, flat.shape, 1) == ay
        mine.append(jnp.sum(jnp.where(pick, flat.astype(F32), 0.0), axis=1, keepdims=True))
    mine = jnp.concatenate(mine, axis=0)
    ids = lax.broadcasted_iota(jnp.int32, (2 * PER, total), 1).astype(F32)
    hot = jnp.where(ids == mine, 1.0, 0.0).astype(BF)
    prior = []
    for b in range(2):
        prow = jnp.zeros((1, members), F32)
        for s in range(PER):
            f = mine[b * PER + s:b * PER + s + 1, :]
            v = jnp.where(place == f, mean_ref[...], 0.0)
            v = jnp.sum(jnp.sum(v, axis=0, keepdims=True), axis=1, keepdims=True)
            prow = prow + jnp.where(lane == ny * s + ay, jnp.broadcast_to(v, (1, members)), 0.0)
        prior.append(prow)
    for b in range(2):
        hi = prior[b].astype(BF).astype(F32)
        rows[2 * b:2 * b + 1, :] = hi
        rows[2 * b + 1:2 * b + 2, :] = prior[b] - hi
    send[2] = rows[0:4, :].astype(BF)
    loads[4].wait()
    rows[...] = mm(hot, cells[...])
    send[0] = rows[0:4, :].astype(BF)
    send[1] = rows[4:8, :].astype(BF)

    pl.semaphore_wait(barrier, ny - 1 + nx - 1)

    own = pltpu.make_async_copy(send, near.at[:, ay], self_sem.at[0])
    own.start()

    def spread_out(o, carry):
        to = lax.rem(ay + o, ny)
        pltpu.make_async_remote_copy(
            send, near.at[:, ay], send_sem.at[to], recv_sem.at[ay],
            device_id=(ax, to), device_id_type=MESH).start()
        return carry

    lax.fori_loop(1, ny, spread_out, 0)
    loads[5].wait()
    loads[6].wait()

    def flatten(ref, bias):
        acc = jnp.zeros((2 * nx, members), F32)
        for s in range(PER):
            spot = jnp.where(lax.broadcasted_iota(jnp.int32, (ny, members), 1)
                             == lax.broadcasted_iota(jnp.int32, (ny, members), 0) + ny * s, 1.0, 0.0)
            acc = acc + exact(ref[:, s, :].astype(F32), spot.astype(F32))
        return acc + bias

    group = lax.rem(lax.broadcasted_iota(jnp.int32, (2 * nx, members), 0), nx)
    strip = lax.rem(lax.broadcasted_iota(jnp.int32, (2 * nx, members), 1), ny)
    meta_ref[0] = flatten(col_ref, (group * cols_x).astype(F32))
    meta_ref[1] = flatten(row_ref, (strip * rows_y).astype(F32))
    meta_ref[2] = flatten(var_ref, 0.0)
    meta_ref[3] = flatten(val_ref, 0.0)

    lam = taper_scale(members)
    inv_sq = (lam / radius) ** 2
    col_x = (ax * cols_x + lax.broadcasted_iota(jnp.int32, (cols_x, 1), 0)).astype(F32)
    ddx = col_x - wide(meta_ref[0, 0:nx, :])
    dx2[...] = ddx * ddx * inv_sq + 1e-30
    columns(meta_ref[0, nx:2 * nx, :], xcol)
    columns(meta_ref[1, nx:2 * nx, :], ycol)

    def cross_tile(i, carry):
        r = pl.ds(pl.multiple_of(i * 128, 128), 128)
        x_c, y_c = xcol[r, :], ycol[r, :]
        for c in range(nx):
            ddx = x_c - meta_ref[0, c:c + 1, :]
            ddy = y_c - meta_ref[1, c:c + 1, :]
            t = (ddx * ddx + ddy * ddy) * inv_sq + 1e-30
            tap_ref[i, :, c * 128:(c + 1) * 128] = taper(t, lam)
        return carry

    def own_tile(n, carry):
        here = (ay * rows_y + n).astype(F32)
        for c in range(nx):
            ddy = here - meta_ref[1, c:c + 1, :]
            t = dx2[:, c * 128:(c + 1) * 128] + ddy * ddy * inv_sq
            tap_ref[nx + n, :, c * 128:(c + 1) * 128] = taper(t, lam)
        return carry

    first, second = SPLIT
    lax.fori_loop(0, nx, cross_tile, 0)
    lax.fori_loop(0, first, own_tile, 0)
    own.wait()

    def arrive(o, carry):
        frm = lax.rem(ay + o, ny)
        pltpu.make_async_remote_copy(
            send, near.at[:, frm], send_sem.at[frm], recv_sem.at[frm],
            device_id=(ax, frm), device_id_type=MESH).wait()
        return carry

    lax.fori_loop(1, ny, arrive, 0)

    keep = pltpu.make_async_copy(near.at[0:2], allz.at[ax], self_sem.at[1])
    keep.start()

    def zout(o, carry):
        to = lax.rem(ax + 2 * o, nx)
        pltpu.make_async_remote_copy(near.at[0:2], allz.at[ax], zsend.at[to], zrecv.at[ax],
                                     device_id=(to, ay), device_id_type=MESH).start()
        return carry

    lax.fori_loop(1, nx // 2, zout, 0)
    pltpu.make_async_remote_copy(near.at[0:2], allz.at[ax], zsend.at[other], zrecv.at[ax],
                                 device_id=(other, ay), device_id_type=MESH).start()
    psum = jnp.sum(near[2].astype(F32), axis=0)
    pnear[0:1, :] = psum[0:1, :] + psum[1:2, :]
    pnear[1:2, :] = psum[2:3, :] + psum[3:4, :]
    allp[ax] = pnear[...]

    def pout(o, carry):
        to = lax.rem(ax + o, nx)
        pltpu.make_async_remote_copy(pnear, allp.at[ax], psend.at[to], precv.at[ax],
                                     device_id=(to, ay), device_id_type=MESH).start()
        return carry

    lax.fori_loop(1, nx, pout, 0)
    lax.fori_loop(first, first + second, own_tile, 0)

    def relay(o, carry):
        g = lax.rem(ax + 2 * o, nx)
        h = g + 1 - 2 * lax.rem(g, 2)
        pltpu.make_async_remote_copy(near.at[0:2], allz.at[g], zsend.at[g], zrecv.at[g],
                                     device_id=(g, ay), device_id_type=MESH).wait()
        pltpu.make_async_remote_copy(allz.at[g], allz.at[g], zsend.at[h], zrecv.at[g],
                                     device_id=(other, ay), device_id_type=MESH).start()
        return carry

    lax.fori_loop(1, nx // 2, relay, 0)
    lax.fori_loop(first + second, rows_y, own_tile, 0)

    def settle(o, carry):
        g = lax.rem(ax + 2 * o, nx)
        h = g + 1 - 2 * lax.rem(g, 2)
        pltpu.make_async_remote_copy(allz.at[h], allz.at[h], zsend.at[h], zrecv.at[h],
                                     device_id=(other, ay), device_id_type=MESH).wait()
        return carry

    lax.fori_loop(0, nx // 2, settle, 0)

    def settle_p(o, carry):
        g = lax.rem(ax + o, nx)
        pltpu.make_async_remote_copy(pnear, allp.at[g], psend.at[g], precv.at[g],
                                     device_id=(g, ay), device_id_type=MESH).wait()
        return carry

    lax.fori_loop(1, nx, settle_p, 0)
    keep.wait()
    p_ref[...] = allp[...]
    for b in range(2):
        z_ref[b] = allz[:, b]


def gather(nx, ny, radius, cols_x, rows_y, spread, mean, col, row, lev, var, val):
    members = spread.shape[1]
    count = nx * ny * PER
    tiles = nx + rows_y
    vm = pl.BlockSpec(memory_space=pltpu.VMEM)
    hbm = pl.BlockSpec(memory_space=pltpu.HBM)
    dma = pltpu.SemaphoreType.DMA
    return pl.pallas_call(
        functools.partial(gather_kernel, nx, ny, radius, cols_x, rows_y),
        out_shape=(pltpu.VMEM((2, nx, ny, PER, members), BF), pltpu.VMEM((nx, 8, members), F32),
                   pltpu.VMEM((4, 2 * nx, members), F32), pltpu.VMEM((tiles, 128, count), F32),
                   pltpu.VMEM(spread.shape, BF), pltpu.VMEM(mean.shape, F32)),
        in_specs=[hbm] * 7,
        out_specs=(vm,) * 6,
        scratch_shapes=[
            pltpu.VMEM(col.shape, jnp.int32),
            pltpu.VMEM(col.shape, jnp.int32),
            pltpu.VMEM(col.shape, jnp.int32),
            pltpu.VMEM(col.shape, F32),
            pltpu.VMEM(col.shape, F32),
            pltpu.VMEM((3, PER, members), BF),
            pltpu.VMEM((8, members), F32),
            pltpu.VMEM((3, ny, PER, members), BF),
            pltpu.VMEM((8, members), F32),
            pltpu.VMEM((nx, 2, ny, PER, members), BF),
            pltpu.VMEM((nx, 8, members), F32),
            pltpu.VMEM((cols_x, count), F32),
            pltpu.VMEM((count, members), F32),
            pltpu.VMEM((count, members), F32),
            dma((7,)), dma((2,)), dma((ny,)), dma((ny,)), dma((nx,)), dma((nx,)), dma((nx,)), dma((nx,)),
        ],
        compiler_params=pltpu.CompilerParams(collective_id=0, has_side_effects=True, vmem_limit_bytes=20 << 20),
    )(*[pltpu.with_memory_space_constraint(a, pltpu.HBM) for a in (spread, mean, col, row, lev, var, val)])


def chain(zx, zt, dcol, z_f32, ivar_row):
    count, members = z_f32.shape
    dof = members - 1.0
    lane = lax.broadcasted_iota(jnp.int32, (count, members), 1)
    d1, d2, d3 = split3(dcol[...])
    zx[:, :members] = z_f32.astype(BF)
    zx[:, members:] = jnp.where(lane == 0, d1.astype(F32), jnp.where(
        lane == 1, d2.astype(F32), jnp.where(lane == 2, d3.astype(F32), 0.0))).astype(BF)
    z_t = z_f32.T
    zt[...] = z_t.astype(BF)
    h1, h2, h3 = split3(z_t * (ivar_row * (1.0 / dof)))
    rhs = zx[...]
    full = mm(jnp.concatenate([h1, h2, h3], axis=0), rhs)
    full = full[:members] + full[members:2 * members] + full[2 * members:]
    row_i = lax.broadcasted_iota(jnp.int32, (members, members), 0)
    col_i = lax.broadcasted_iota(jnp.int32, (members, members), 1)
    eye = jnp.where(row_i == col_i, 1.0, 0.0).astype(F32)
    gram = full[:, :members] + eye
    vec = jnp.broadcast_to(jnp.sum(full[:, members:], axis=1, keepdims=True), (members, members))

    square = exact(gram, gram)
    top = jnp.sqrt(jnp.max(jnp.sum(jnp.abs(square), axis=1, keepdims=True), axis=0, keepdims=True))
    scale = 2.0 / (1.0 + top)
    resid = eye - 2.0 * scale * gram + scale * scale * square
    inv = scale * (2.0 * eye - scale * gram)
    for _ in range(DOUBLINGS):
        both = mm3(jnp.concatenate([inv, resid], axis=0), resid)
        inv = inv + both[:members]
        resid = both[members:]
    inv = inv + mm3(inv, resid)
    return gram, vec, inv


def chain_end(zx, qx, ivcol, gram, vec, inv):
    members = gram.shape[0]
    rhs = zx[...]
    eye = jnp.where(lax.broadcasted_iota(jnp.int32, gram.shape, 0)
                    == lax.broadcasted_iota(jnp.int32, gram.shape, 1), 1.0, 0.0).astype(F32)

    def more(state):
        step, miss, _ = state
        return jnp.logical_and(step < 60, miss > 1e-2)

    def newton(state):
        step, _, x = state
        resid = eye - exact(gram, x)
        x = x + exact(x, resid)
        return step + 1, jnp.max(jnp.sum(jnp.abs(resid), axis=1, keepdims=True)), x

    _, _, inv = lax.while_loop(more, newton, (jnp.int32(0), jnp.float32(1.0), inv))
    w = exact(inv, vec)
    r1, r2, r3 = split3(jnp.concatenate([inv, -w], axis=1))
    row_e = lax.broadcasted_iota(jnp.int32, (members, 2 * members), 0)
    col_e = lax.broadcasted_iota(jnp.int32, (members, 2 * members), 1)
    ones = jnp.where(jnp.logical_and(row_e < 3, col_e >= members), 1.0, 0.0).astype(BF)
    z_b = rhs[:, :members]
    acc = mm(rhs, jnp.concatenate([r1, ones], axis=0)) + mm(
        jnp.concatenate([z_b, z_b], axis=1), jnp.concatenate([r2, r3], axis=0))
    iv = ivcol[...]
    qx[...] = (acc * jnp.concatenate([iv, iv], axis=1)).astype(BF)


def update_kernel(nx, ny, radius, step_y, spread_ref, mean_ref, z_ref, p_ref, meta_ref, tap, mean_out, spread_hbm,
                  spread_out, out_sem, zx, zt, qx, zf, z1, dcol, ivcol, macc, gain, dx2, ahead):
    levels, rows_y, cols_x, members = spread_out.shape
    count = z1.shape[0]
    unit = -1.0

    def panel(b):
        zf[...] = z_ref[b].astype(F32).reshape(count, members)
        group = ny * PER
        return jnp.concatenate([zf[pl.ds(i * group + s, ny, stride=PER), :]
                                for i in range(nx) for s in range(PER)], axis=0)

    def rows8(q, b):
        return meta_ref[q, b * nx:(b + 1) * nx, :]

    def gap(b):
        return rows8(3, b) - jnp.concatenate([p_ref[i, b:b + 1, :] for i in range(nx)], axis=0)

    columns(gap(0), dcol)
    columns(1.0 / rows8(2, 0), ivcol)
    state = chain(zx, zt.at[0], dcol, panel(0), wide(1.0 / rows8(2, 0)))
    chain_end(zx, qx.at[0], ivcol, *state)
    columns(gap(1), dcol)
    columns(1.0 / rows8(2, 1), ivcol)
    z1[...] = panel(1).astype(BF)

    def cross_fill(c):
        for i in range(count // 256):
            cut = slice(i * 256, (i + 1) * 256)
            cov = mm(z1[c * 512:(c + 1) * 512, :], zt[0, :, cut])
            gain[c % 2, 0:512, cut] = (tap[4 * c:4 * c + 4, :, cut].reshape(512, 256) * cov).astype(BF)

    def cross_drain(c):
        r = slice(c * 512, (c + 1) * 512)
        inc = mm(gain[c % 2, 0:512, :], qx[0])
        z1[r, :] = (z1[r, :].astype(F32) - (0.5 * unit) * inc[:, :members]).astype(BF)
        dcol[r, :] = dcol[r, :] - unit * inc[:, members:]

    for c in range(count // 512 + 1):
        if c > 0:
            cross_drain(c - 1)
        if c < count // 512:
            cross_fill(c)
    state = chain(zx, zt.at[1], dcol, z1[...].astype(F32), wide(1.0 / rows8(2, 1)))
    chain_end(zx, qx.at[1], ivcol, *state)

    macc[...] = jnp.zeros_like(macc)
    lane = lax.broadcasted_iota(jnp.int32, (cols_x, members), 1)
    part = step_y * cols_x
    lam = taper_scale(members)
    inv_sq = (lam / radius) ** 2
    col_x = (lax.axis_index("gx") * cols_x + lax.broadcasted_iota(jnp.int32, (cols_x, 1), 0)).astype(F32)
    ddx = col_x - wide(meta_ref[0, nx:2 * nx, :])
    dx2[...] = ddx * ddx * inv_sq + 1e-30
    base_y = lax.axis_index("gy") * rows_y

    def taper_rows(y, cut):
        out = []
        for c in range(cut.start // 128, cut.stop // 128):
            ddy = (base_y + y).astype(F32) - meta_ref[1, nx + c:nx + c + 1, :]
            out.append(taper(dx2[:, c * 128:(c + 1) * 128] + ddy * ddy * inv_sq, lam))
        return jnp.concatenate(out, axis=1)

    steps = rows_y // step_y

    def rows_of(n):
        return slice((n % steps) * step_y, (n % steps + 1) * step_y)

    def spread_at(n):
        ref = spread_ref if n < steps else spread_out
        return ref[:, rows_of(n)].reshape(levels * part, members)

    def fill(n):
        b, y = n // steps, (n % steps) * step_y
        slot = gain.at[n % 2]
        s = spread_at(n)
        for i in range(count // 256):
            cut = slice(i * 256, (i + 1) * 256)
            cov = mm(s, zt[b, :, cut])
            if b == 0:
                t = tap[nx + y:nx + y + step_y, :, cut].reshape(part, 256)
            else:
                t = ahead[y:y + step_y, :, cut].reshape(part, 256)
            for lev in range(levels):
                slot[lev * part:(lev + 1) * part, cut] = (t * cov[lev * part:(lev + 1) * part]).astype(BF)

    def drain(n):
        b, y = n // steps, (n % steps) * step_y
        inc = mm(gain[n % 2], qx[b])
        new = (spread_at(n).astype(F32) - (0.5 * unit) * inc[:, :members]).astype(BF)
        spread_out[:, rows_of(n)] = new.reshape(levels, step_y, cols_x, members)
        if b == 1:
            pltpu.make_async_copy(spread_out.at[:, rows_of(n)], spread_hbm.at[:, rows_of(n)], out_sem).start()
        acc = macc[...]
        for lev in range(levels):
            for k in range(step_y):
                at = (lev * step_y + k) * cols_x
                acc = acc + jnp.where(lane == lev * rows_y + y + k, inc[at:at + cols_x, members:], 0.0)
        macc[...] = acc

    def look_ahead(y):
        for i in range(count // 256):
            cut = slice(i * 256, (i + 1) * 256)
            ahead[y, :, cut] = taper_rows(jnp.int32(y), cut)

    done = 0
    for n in range(2 * steps + 1):
        if n > 0:
            drain(n - 1)
        if n < 2 * steps:
            fill(n)
        goal = min(rows_y, LEAD + (n + 1) * rows_y // (2 * steps))
        for y in range(done, goal):
            look_ahead(y)
        done = goal
    pltpu.make_async_copy(spread_out, spread_hbm, out_sem).wait()
    mean_out[...] = mean_ref[...] + unit * macc[...].T[:levels * rows_y, :]


def update(nx, ny, radius, step_y, spread, mean, z, p, meta, tap):
    levels, rows_y, cols_x, members = spread.shape
    count = tap.shape[2]
    vm = pl.BlockSpec(memory_space=pltpu.VMEM)
    return pl.pallas_call(
        functools.partial(update_kernel, nx, ny, radius, step_y),
        out_shape=(jax.ShapeDtypeStruct(mean.shape, F32), jax.ShapeDtypeStruct(spread.shape, BF)),
        in_specs=[vm] * 6,
        out_specs=(vm, pl.BlockSpec(memory_space=pltpu.HBM)),
        scratch_shapes=[
            pltpu.VMEM(spread.shape, BF),
            pltpu.SemaphoreType.DMA,
            pltpu.VMEM((count, 2 * members), BF),
            pltpu.VMEM((2, members, count), BF),
            pltpu.VMEM((2, count, 2 * members), BF),
            pltpu.VMEM((count, members), F32),
            pltpu.VMEM((count, members), BF),
            pltpu.VMEM((count, members), F32),
            pltpu.VMEM((count, members), F32),
            pltpu.VMEM((cols_x, members), F32),
            pltpu.VMEM((2, levels * step_y * cols_x, count), BF),
            pltpu.VMEM((cols_x, count), F32),
            pltpu.VMEM((rows_y, cols_x, count), F32),
        ],
        compiler_params=pltpu.CompilerParams(vmem_limit_bytes=34 << 20),
    )(spread, mean, z, p, meta, tap)


def body(state_mean, state_spread, obs_value, obs_var, obs_col, obs_row, obs_level):
    levels, rows_y, cols_x, members = state_spread.shape
    nx, ny = lax.axis_size("gx"), lax.axis_size("gy")
    radius = nx * cols_x // 2
    spread = state_spread.reshape(levels * rows_y * cols_x, members)
    mean = state_mean.reshape(levels * rows_y, cols_x)

    def turn(a):
        return jnp.transpose(a, (0, 1, 3, 2)).reshape(2 * nx, PER, ny)

    z, p, meta, tap, cells, mean = gather(nx, ny, radius, cols_x, rows_y, spread, mean, turn(obs_col), turn(obs_row),
                             turn(obs_level), turn(obs_var), turn(obs_value))
    new_mean, new_spread = update(nx, ny, radius, STEP_Y, cells.reshape(state_spread.shape), mean, z, p, meta, tap)
    return new_mean.reshape(state_mean.shape), new_spread


def solution(mesh):
    return jax.shard_map(
        body,
        mesh=mesh,
        in_specs=(P(None, "gy", "gx"), P(None, "gy", "gx", None), P(), P(), P(), P(), P()),
        out_specs=(P(None, "gy", "gx"), P(None, "gy", "gx", None)),
        check_vma=False,
    )
```
